256 devices in a mesh: dp: 8 (over z), seq: 32 (over x, y, core).
Axes of the slice: x: 4, y: 4, z: 8, core: 2. Of those that a mesh axis runs over, the one named last changes fastest.
Arguments:
- hidden: bfloat16 [32768, 5120], P(('dp', 'seq')), may hold values from -24 to 24
- queries: bfloat16 [32768, 4096], P(('dp', 'seq')), may hold values from -330 to 330
- key_states: bfloat16 [32768, 4096], P(('dp', 'seq')), may hold values from -18 to 18
- value_states: bfloat16 [32768, 4096], P(('dp', 'seq')), may hold values from -6 to 6
- attention_out: bfloat16 [32768, 4096], P(('dp', 'seq')), may hold values from -6 to 6
- grad_out: bfloat16 [32768, 4096], P(('dp', 'seq')), may hold values from -24 to 24
- lengths: int32 [8, 4], P('dp'), may hold values from 1 to 2048, 4096 in all within a row
- down_query: bfloat16 [8, 5120], replicated, may hold values from -0.00048828125 to 0.00048828125
- up_query: bfloat16 [8, 4096], replicated, may hold values from -0.00048828125 to 0.00048828125
- down_value: bfloat16 [8, 5120], replicated, may hold values from -0.00048828125 to 0.00048828125
- up_value: bfloat16 [8, 4096], replicated, may hold values from -0.00048828125 to 0.00048828125
Outputs:
- grad_queries: bfloat16 [32768, 4096], P(('dp', 'seq'))
- grad_keys: bfloat16 [32768, 4096], P(('dp', 'seq'))
- value_gradients: bfloat16 [32768, 4096], P(('dp', 'seq'))
- query_down_gradient: float32 [8, 5120], P(None, 'dp')
- query_up_gradient: float32 [8, 4096], P(None, 'dp')
- value_down_gradient: float32 [8, 5120], P(None, 'dp')
- value_up_gradient: float32 [8, 4096], P(None, 'dp')
The draws below stay inside these ranges and needn't reach their ends.
Inputs may be any that keep to these rules, and one draw needn't show every extreme that they name: Each row lists the lengths of the 4 sequences of one pack in packing order; a row sums to 4096.
All inputs are finite; a program needn't handle non-finite values.
Results may differ from the reference program's by a relative error of at most 0.0067.
Values may be sent and summed in bfloat16 or wider, within the bound.
A program may use at most 64 MiB of HBM per device.

```python
import math
import jax
import jax.numpy as jnp
import numpy as np
from jax import lax

D = 5120
H = 32
HD = 128
ADAPTER_RANK = 8
ADAPTER_ALPHA = 16
NSEQ = 4
S = 4096
TOKENS = 32768
HH = 4096
N_DP = 8


def query_key_pair(key):
    base_key = jax.random.fold_in(key, 7)
    key_query, key_keys = jax.random.split(base_key, 2)
    queries = jnp.clip(jax.random.normal(key_query, (TOKENS, HH), jnp.float32), -6.0, 6.0)
    keys_drawn = jnp.clip(jax.random.normal(key_keys, (TOKENS, HH), jnp.float32), -6.0, 6.0)
    return (queries, keys_drawn)


def draw_queries(key, part):
    return query_key_pair(key)[0].astype(jnp.bfloat16)


def draw_key_states(key, part):
    return query_key_pair(key)[1].astype(jnp.bfloat16)


def spiked(entries, rng, source, target, blocks, factor):
    owner, partner = [(jnp.arange(entries.shape[position]) // (entries.shape[position] // blocks)).reshape([-1 if axis == position else 1 for axis in range(entries.ndim)]) for position in (source, target)]
    chosen = jax.random.permutation(rng, blocks)[partner]
    strong = (owner == chosen) | (owner == (partner + blocks // 2) % blocks)
    return jnp.where(strong, factor * entries, entries)


def steps_of(stream_key, shape, cuts, smallest, high):
    def one(axis_at, parts):
        heights = jax.random.uniform(jax.random.fold_in(jax.random.fold_in(stream_key, 6), axis_at), (parts,), jnp.float32, smallest / len(cuts), high / len(cuts))
        return jnp.repeat(jnp.exp(heights), shape[axis_at] // parts).reshape((-1,) + (1,) * (len(shape) - axis_at - 1))

    level = one(*cuts[0])
    for cut in cuts[1:]:
        level = level * one(*cut)
    return level


def split_up(number_of, total, reach, lean):
    loads = [(1 << 20) // math.isqrt(standing ** lean) + 1 for standing in range(2, number_of + 1)]
    spare, given = total - reach - (number_of - 1), [1] * (number_of - 1)
    while spare > 0:
        free = [i for i in range(number_of - 1) if given[i] < reach]
        mass, budget = sum([loads[i] for i in free]), spare
        for i in free:
            extra = min(reach - given[i], max(1, budget * loads[i] // mass), spare)
            given[i] = given[i] + extra
            spare = spare - extra
    return np.array([reach] + given)


def ragged(own_key, number_of, total, reach, lean):
    if number_of == 2:
        one = jax.random.randint(own_key, (), max(1, total - reach), min(reach, total - 1) + 1)
        return jnp.stack([one, total - one])
    sizes = jnp.asarray(split_up(number_of, total, reach, lean), jnp.int32)
    twos = (number_of - 1) // 2
    source_of, sink = sizes[1:1 + 2 * twos:2], sizes[2:2 + 2 * twos:2]
    room = jnp.minimum(source_of - 1, reach - sink)
    shifted = jax.random.randint(jax.random.fold_in(own_key, 1), (twos,), 0, 1 << 20) % (room + 1)
    sizes = sizes.at[1:1 + 2 * twos:2].set(source_of - shifted).at[2:2 + 2 * twos:2].set(sink + shifted)
    return sizes[jax.random.permutation(jax.random.fold_in(own_key, 2), number_of)]


def gaussian(rng, dims, scale, most, cuts=(), kind=jnp.bfloat16):
    loudness = steps_of(rng, dims, cuts, -0.22, 0.18) if cuts else 1.0
    values = jax.random.normal(rng, dims, jnp.float32) * scale * loudness
    return jnp.minimum(jnp.maximum(values, -most), most).astype(kind)


def noise_with(rng, extent, width, most, pieces, heavy, kind=jnp.bfloat16):
    entries = width * jax.random.normal(rng, extent, jnp.float32)
    if pieces:
        entries = entries * steps_of(rng, extent, pieces, -0.22, 0.18)
    return jnp.clip(spiked(entries, jax.random.fold_in(rng, 3), *heavy), -most, most).astype(kind)


def setup_inputs(seed: int = 0) -> dict:
    key_of = jax.random.split(jax.random.key(seed), 12)
    hidden = noise_with(key_of[0], (TOKENS, D), 1.0, 24.0, ((0, 256),), (0, 1, 256, 6.0))
    queries = draw_queries(jax.random.fold_in(key_of[11], 71), 0)
    key_states = draw_key_states(jax.random.fold_in(key_of[11], 71), 0)
    value_states = gaussian(key_of[3], (TOKENS, HH), 1.0, 6.0, ((0, 256),))
    attention_out = gaussian(key_of[4], (TOKENS, HH), 1.0, 6.0, ((0, 256),))
    grad_out = noise_with(key_of[5], (TOKENS, HH), 1.0, 24.0, ((0, 256),), (0, 1, 256, 6.0))
    lengths = jax.vmap(lambda own: ragged(own, NSEQ, S, S // 2, 2))(jax.random.split(key_of[6], N_DP)).reshape((N_DP, NSEQ)).astype(jnp.int32)
    down_query = gaussian(key_of[7], (ADAPTER_RANK, D), (D * TOKENS) ** -0.5, 0.00048828125)
    up_query = gaussian(key_of[8], (ADAPTER_RANK, HH), (HH * TOKENS) ** -0.5, 0.00048828125)
    down_value = gaussian(key_of[9], (ADAPTER_RANK, D), (D * TOKENS) ** -0.5, 0.00048828125)
    up_value = gaussian(key_of[10], (ADAPTER_RANK, HH), (HH * TOKENS) ** -0.5, 0.00048828125)
    return {"hidden": hidden, "queries": queries, "key_states": key_states, "value_states": value_states, "attention_out": attention_out, "grad_out": grad_out, "lengths": lengths, "down_query": down_query, "up_query": up_query, "down_value": down_value, "up_value": up_value}


def pack_begin(lengths_row, total):
    seq_ends = jnp.cumsum(lengths_row).astype(jnp.int32)
    starts = (seq_ends - lengths_row).astype(jnp.int32)
    positions = jnp.arange(total, dtype=jnp.int32)
    inside = (positions[:, None] >= starts[None, :]) & (positions[:, None] < seq_ends[None, :])
    return lax.optimization_barrier(jnp.sum(jnp.where(inside, starts[None, :], 0), axis=1)).astype(jnp.int32)

def rotate_back(grads, seq_positions):
    rows = grads.shape[0]
    half = HD // 2
    inverse = jnp.exp(-(jnp.arange(half, dtype=jnp.float32) * (2.0 / HD)) * math.log(10000.0))
    angles = seq_positions.astype(jnp.float32)[:, None] * inverse[None, :]
    cosine = jnp.cos(angles)[:, None, :]
    sine = jnp.sin(angles)[:, None, :]
    split = grads.astype(jnp.float32).reshape(rows, H, HD)
    first = split[:, :, :half]
    second = split[:, :, half:]
    new_first = first * cosine + second * sine
    new_second = second * cosine - first * sine
    joined = jnp.concatenate([new_first, new_second], axis=2)
    return joined.reshape(rows, H * HD).astype(jnp.bfloat16)

def head_grads(operands, begin):
    head_query, head_key, head_value, head_out, head_grad = operands
    total = head_query.shape[0]
    scaling = 1.0 / math.sqrt(HD)
    positions = jnp.arange(total, dtype=jnp.int32)
    allowed = (positions[None, :] >= begin[:, None]) & (positions[None, :] <= positions[:, None])
    scores = jnp.dot(head_query, head_key.T, preferred_element_type=jnp.float32) * scaling
    masked = jnp.where(allowed, scores, -1e+30)
    row_top = lax.optimization_barrier(jnp.max(masked, axis=1, keepdims=True))
    weights = jnp.where(allowed, jnp.exp(masked - row_top), 0.0)
    prob_rows = weights / lax.optimization_barrier(jnp.sum(weights, axis=1, keepdims=True))
    prob_low = prob_rows.astype(jnp.bfloat16)
    grad_prob = jnp.dot(head_grad, head_value.T, preferred_element_type=jnp.float32)
    row_delta = lax.optimization_barrier(jnp.sum(head_out.astype(jnp.float32) * head_grad.astype(jnp.float32), axis=1, keepdims=True))
    grad_score = (prob_rows * (grad_prob - row_delta)).astype(jnp.bfloat16)
    grad_query = (jnp.dot(grad_score, head_key, preferred_element_type=jnp.float32) * scaling).astype(jnp.bfloat16)
    grad_key = (jnp.dot(grad_score.T, head_query, preferred_element_type=jnp.float32) * scaling).astype(jnp.bfloat16)
    grad_value = jnp.dot(prob_low.T, head_grad, preferred_element_type=jnp.float32).astype(jnp.bfloat16)
    return (grad_query, grad_key, grad_value)

def pack_grads(operands):
    pack_query, pack_key, pack_value, pack_out, pack_grad, lengths_row = operands
    total = pack_query.shape[0]
    begin = pack_begin(lengths_row, total)

    def split_heads(array):
        return array.reshape(total, H, HD).transpose(1, 0, 2)

    def one_head(head_operands):
        return head_grads(head_operands, begin)
    split_inputs = (split_heads(pack_query), split_heads(pack_key), split_heads(pack_value), split_heads(pack_out), split_heads(pack_grad))
    grad_query, grad_key, grad_value = lax.map(one_head, split_inputs)

    def join_heads(array):
        return array.transpose(1, 0, 2).reshape(total, H * HD)
    seq_positions = (jnp.arange(total, dtype=jnp.int32) - begin).astype(jnp.int32)
    return (join_heads(grad_query), join_heads(grad_key), join_heads(grad_value), seq_positions)

def reference(hidden, queries, key_states, value_states, attention_out, grad_out, lengths, down_query, up_query, down_value, up_value):

    def packed(array):
        return array.reshape(N_DP, S, H * HD)
    grad_queries, grad_keys, value_gradients, seq_positions = lax.map(pack_grads, (packed(queries), packed(key_states), packed(value_states), packed(attention_out), packed(grad_out), lengths))
    grad_queries = grad_queries.reshape(TOKENS, H * HD)
    grad_keys = grad_keys.reshape(TOKENS, H * HD)
    value_gradients = value_gradients.reshape(TOKENS, H * HD)
    seq_positions = seq_positions.reshape(TOKENS)
    query_gradient_before = rotate_back(grad_queries, seq_positions)
    adapter_scale = ADAPTER_ALPHA / ADAPTER_RANK
    query_lowrank = jnp.dot(hidden, down_query.T, preferred_element_type=jnp.float32).astype(jnp.bfloat16)
    value_lowrank = jnp.dot(hidden, down_value.T, preferred_element_type=jnp.float32).astype(jnp.bfloat16)
    query_backprop = jnp.dot(query_gradient_before, up_query.T, preferred_element_type=jnp.float32).astype(jnp.bfloat16)
    value_backprop = jnp.dot(value_gradients, up_value.T, preferred_element_type=jnp.float32).astype(jnp.bfloat16)
    query_down_gradient = adapter_scale * jnp.dot(query_backprop.T, hidden, preferred_element_type=jnp.float32)
    query_up_gradient = adapter_scale * jnp.dot(query_lowrank.T, query_gradient_before, preferred_element_type=jnp.float32)
    value_down_gradient = adapter_scale * jnp.dot(value_backprop.T, hidden, preferred_element_type=jnp.float32)
    value_up_gradient = adapter_scale * jnp.dot(value_lowrank.T, value_gradients, preferred_element_type=jnp.float32)
    return (grad_queries, grad_keys, value_gradients, query_down_gradient, query_up_gradient, value_down_gradient, value_up_gradient)
```

```python
import math

import jax
import jax.numpy as jnp
from jax import lax
from jax.experimental import pallas as pl
from jax.experimental.pallas import tpu as pltpu
from jax.sharding import PartitionSpec as P

H = 32
HD = 128
RANK = 8
ADAPTER_SCALE = 2.0
BQ = 256
BK = 256
MESH = pl.DeviceIdType.MESH
NT = (((1,), (1,)), ((), ()))
F32 = jnp.float32
BF16 = jnp.bfloat16


def nt_dot(a, b):
    return lax.dot_general(a, b, NT, preferred_element_type=F32)


def starts_of(len_ref):
    first = len_ref[0, 0]
    second = first + len_ref[0, 1]
    third = second + len_ref[0, 2]
    return first, second, third


def begin_of(positions, starts):
    found = jnp.zeros_like(positions)
    for start in starts:
        found = jnp.where(positions >= start, start, found)
    return found


def partner(me, step):
    return lax.rem(me + step, 32)


def gather_kernel(q_ref, k_ref, v_ref, g_ref, o_ref, hq, hk, hv, hg, hd, g_buf, o_buf, d_buf, send, recv, local, load):
    members = 32
    me = lax.axis_index("seq")
    rows = q_ref.shape[0]
    barrier = pltpu.get_barrier_semaphore()

    def greet(step, _):
        pl.semaphore_signal(barrier, inc=1, device_id={"seq": partner(me, step)}, device_id_type=MESH)
        return 0

    lax.fori_loop(1, members, greet, 0)
    load_g = pltpu.make_async_copy(g_ref, g_buf, load.at[0])
    load_o = pltpu.make_async_copy(o_ref, o_buf, load.at[1])
    load_g.start()
    load_o.start()
    pairs = ((q_ref, hq), (k_ref, hk), (v_ref, hv), (g_ref, hg))
    my_rows = pl.ds(pl.multiple_of(me * rows, rows), rows)

    def columns(member):
        return pl.ds(pl.multiple_of(member * HD, HD), HD)

    own = [
        pltpu.make_async_copy(src.at[:, columns(me)], dst.at[my_rows, :], local.at[index])
        for index, (src, dst) in enumerate(pairs)
    ]
    for copy in own:
        copy.start()
    pl.semaphore_wait(barrier, members - 1)

    def remote(index, step):
        src, dst = pairs[index]
        other = partner(me, step)
        return pltpu.make_async_remote_copy(
            src_ref=src.at[:, columns(other)],
            dst_ref=dst.at[my_rows, :],
            send_sem=send.at[index, step],
            recv_sem=recv.at[index, step],
            device_id={"seq": other},
            device_id_type=MESH,
        )

    def remote_delta(step):
        other = partner(me, step)
        return pltpu.make_async_remote_copy(
            src_ref=d_buf.at[other],
            dst_ref=hd.at[me],
            send_sem=send.at[4, step],
            recv_sem=recv.at[4, step],
            device_id={"seq": other},
            device_id_type=MESH,
        )

    def start_all(step, _):
        for index in range(4):
            remote(index, step).start()
        return 0

    lax.fori_loop(1, members, start_all, 0)
    load_g.wait()
    load_o.wait()

    def delta_of(head, _):
        cols = columns(head)
        product = g_buf[:, cols].astype(F32) * o_buf[:, cols].astype(F32)
        d_buf[head] = jnp.sum(product.T, axis=0, keepdims=True)
        return 0

    lax.fori_loop(0, H, delta_of, 0)
    own_delta = pltpu.make_async_copy(d_buf.at[me], hd.at[me], local.at[4])
    own_delta.start()

    def start_delta(step, _):
        remote_delta(step).start()
        return 0

    lax.fori_loop(1, members, start_delta, 0)
    for copy in own:
        copy.wait()
    own_delta.wait()

    def finish(step, _):
        for index in range(4):
            remote(index, step).wait()
        remote_delta(step).wait()
        return 0

    lax.fori_loop(1, members, finish, 0)


def gather_heads(queries, key_states, value_states, grad_out, attention_out):
    rows, width = queries.shape
    anywhere = pl.BlockSpec(memory_space=pl.ANY)
    total = rows * 32
    head = jax.ShapeDtypeStruct((total, HD), BF16)
    return pl.pallas_call(
        gather_kernel,
        name="gather_heads",
        out_shape=(head, head, head, head, jax.ShapeDtypeStruct((32, 1, rows), F32)),
        in_specs=[anywhere] * 5,
        out_specs=[anywhere] * 5,
        scratch_shapes=[
            pltpu.VMEM((rows, width), BF16),
            pltpu.VMEM((rows, width), BF16),
            pltpu.VMEM((H, 1, rows), F32),
            pltpu.SemaphoreType.DMA((5, 32)),
            pltpu.SemaphoreType.DMA((5, 32)),
            pltpu.SemaphoreType.DMA((5,)),
            pltpu.SemaphoreType.DMA((2,)),
        ],
        compiler_params=pltpu.CompilerParams(
            collective_id=0, has_side_effects=True, vmem_limit_bytes=16 << 20
        ),
    )(queries, key_states, value_states, grad_out, attention_out)


def attention_kernel(len_ref, q_ref, k_ref, v_ref, g_ref, d_ref, dq_ref, dk_ref, dv_ref, kt, w_buf, t_buf, dk_acc, dv_acc, stat):
    total = q_ref.shape[0]
    starts = starts_of(len_ref)
    scaling = 1.0 / math.sqrt(HD)
    to_log2 = scaling * math.log2(math.e)
    dk_acc[...] = jnp.zeros_like(dk_acc)
    dv_acc[...] = jnp.zeros_like(dv_acc)

    def turn(block, _):
        at = pl.multiple_of(block * 256, 256)
        kt[:, pl.ds(at, 256)] = k_ref[pl.ds(at, 256), :].T
        return 0

    lax.fori_loop(0, total // 256, turn, 0)

    def fold(x, op):
        return op(x.reshape(x.shape[0] // 8, 8, x.shape[1]), axis=0)

    def outer(query_block, _):
        q0 = pl.multiple_of(query_block * BQ, BQ)
        q_rows = q_ref[pl.ds(q0, BQ), :]
        g_rows = g_ref[pl.ds(q0, BQ), :]
        delta = jnp.concatenate([d_ref[query_block * (BQ // 128) + i] for i in range(BQ // 128)], axis=1)
        query_at = q0 + lax.broadcasted_iota(jnp.int32, (1, BQ), 1)
        query_begin = begin_of(query_at, starts)
        low = begin_of(q0, starts)
        high = begin_of(q0 + (BQ - 1), starts)
        first = lax.div(low, BK)
        last = lax.div(q0 + (BQ - 1), BK) + 1
        stat[0] = jnp.full((8, BQ), -1e30, F32)

        def score(key_block, _):
            k0 = pl.multiple_of(key_block * BK, BK)
            rows = pl.ds(k0, BK)
            inside = jnp.logical_and(high <= k0, k0 + (BK - 1) <= q0)

            @pl.when(inside)
            def _():
                s = nt_dot(k_ref[rows, :], q_rows)
                w_buf[rows, :] = s
                stat[0] = jnp.maximum(stat[0], fold(s, jnp.max))

            @pl.when(jnp.logical_not(inside))
            def _():
                key_at = k0 + lax.broadcasted_iota(jnp.int32, (BK, BQ), 0)
                allowed = jnp.logical_and(key_at >= query_begin, key_at <= query_at)
                s = jnp.where(allowed, nt_dot(k_ref[rows, :], q_rows), -1e30)
                w_buf[rows, :] = s
                stat[0] = jnp.maximum(stat[0], fold(s, jnp.max))

            return 0

        lax.fori_loop(first, last, score, 0)
        top = jnp.max(stat[0], axis=0, keepdims=True)
        stat[1] = jnp.zeros((8, BQ), F32)

        def weigh(key_block, _):
            rows = pl.ds(pl.multiple_of(key_block * BK, BK), BK)
            w = jnp.exp2((w_buf[rows, :] - top) * to_log2)
            stat[1] = stat[1] + fold(w, jnp.sum)
            w_buf[rows, :] = w
            t_buf[rows, :] = w * (nt_dot(v_ref[rows, :], g_rows) - delta)
            return 0

        lax.fori_loop(first, last, weigh, 0)
        inverse = 1.0 / jnp.sum(stat[1], axis=0, keepdims=True)

        def spread(key_block, dq):
            k0 = pl.multiple_of(key_block * BK, BK)
            rows = pl.ds(k0, BK)
            p = (w_buf[rows, :] * inverse).astype(BF16)
            ds = (t_buf[rows, :] * inverse).astype(BF16)
            dv_acc[rows, :] += jnp.dot(p, g_rows, preferred_element_type=F32)
            dk_acc[rows, :] += jnp.dot(ds, q_rows, preferred_element_type=F32)
            return dq + jnp.dot(kt[:, rows], ds, preferred_element_type=F32)

        dq = lax.fori_loop(first, last, spread, jnp.zeros((HD, BQ), F32))
        dq_ref[pl.ds(q0, BQ), :] = (dq * scaling).T.astype(BF16)
        return 0

    lax.fori_loop(0, total // BQ, outer, 0)
    dk_ref[...] = (dk_acc[...] * scaling).astype(BF16)
    dv_ref[...] = dv_acc[...].astype(BF16)


def attention_backward(lengths, q, k, v, g, delta):
    total = q.shape[0]
    vmem = pl.BlockSpec(memory_space=pltpu.VMEM)
    head = jax.ShapeDtypeStruct((total, HD), BF16)
    return pl.pallas_call(
        attention_kernel,
        name="attention_backward",
        out_shape=(head, head, head),
        in_specs=[pl.BlockSpec(memory_space=pltpu.SMEM)] + [vmem] * 5,
        out_specs=[vmem] * 3,
        scratch_shapes=[
            pltpu.VMEM((HD, total), BF16),
            pltpu.VMEM((total, BQ), F32),
            pltpu.VMEM((total, BQ), F32),
            pltpu.VMEM((total, HD), F32),
            pltpu.VMEM((total, HD), F32),
            pltpu.VMEM((2, 8, BQ), F32),
        ],
        compiler_params=pltpu.CompilerParams(vmem_limit_bytes=48 << 20),
    )(lengths, q, k, v, g, delta)


def adapter_kernel(
    len_ref, dq_ref, dk_ref, dv_ref, hid_ref, downq, upq, downv, upv,
    gq_ref, gk_ref, gv_ref, qd_ref, qu_ref, vd_ref, vu_ref,
    q_in, v_in, turned, hid, part, z_in, tiles, r_in, done,
    send, recv, local, load, z_send, z_recv, r_send, r_recv, a_send, a_recv,
):
    members, groups = 32, 8
    me = lax.axis_index("seq")
    dp = lax.axis_index("dp")
    rows, width = q_in.shape
    model = hid.shape[1]
    d_cols = model // groups
    u_cols = width // groups
    d_tiles = d_cols // 128
    u_tiles = u_cols // 128
    n_tiles = 2 * (d_tiles + u_tiles)
    barrier = pltpu.get_barrier_semaphore()

    def across(step):
        return lax.rem(dp + step, groups)

    def greet(step, _):
        pl.semaphore_signal(barrier, inc=1, device_id={"seq": partner(me, step)}, device_id_type=MESH)
        return 0

    def greet_group(step, _):
        pl.semaphore_signal(barrier, inc=1, device_id={"dp": across(step)}, device_id_type=MESH)
        return 0

    lax.fori_loop(1, members, greet, 0)
    lax.fori_loop(1, groups, greet_group, 0)
    load_hid = pltpu.make_async_copy(hid_ref, hid, load.at[0])
    load_hid.start()
    pairs = ((dq_ref, q_in), (dv_ref, v_in), (dk_ref, gk_ref))
    my_cols = pl.ds(pl.multiple_of(me * HD, HD), HD)

    def rows_of(member):
        return pl.ds(pl.multiple_of(member * rows, rows), rows)

    own = [
        pltpu.make_async_copy(src.at[rows_of(me), :], dst.at[:, my_cols], local.at[index])
        for index, (src, dst) in enumerate(pairs)
    ]
    for copy in own:
        copy.start()
    pl.semaphore_wait(barrier, members - 1 + groups - 1)

    def remote(index, step):
        src, dst = pairs[index]
        other = partner(me, step)
        return pltpu.make_async_remote_copy(
            src_ref=src.at[rows_of(other), :],
            dst_ref=dst.at[:, my_cols],
            send_sem=send.at[index, step],
            recv_sem=recv.at[index, step],
            device_id={"seq": other},
            device_id_type=MESH,
        )

    for index in range(3):
        def start_one(step, _, index=index):
            remote(index, step).start()
            return 0

        lax.fori_loop(1, members, start_one, 0)

    load_hid.wait()
    low_q = nt_dot(downq[...], hid[...]).astype(BF16)
    low_v = nt_dot(downv[...], hid[...]).astype(BF16)
    token = me * rows + lax.broadcasted_iota(jnp.int32, (rows, HD), 0)
    place = (token - begin_of(token, starts_of(len_ref))).astype(F32)
    lane = lax.broadcasted_iota(jnp.int32, (rows, HD), 1)
    pair = jnp.where(lane >= HD // 2, lane - HD // 2, lane).astype(F32)
    angle = place * jnp.exp(-(pair * (2.0 / HD)) * math.log(10000.0))
    cosine = jnp.cos(angle)
    sine = jnp.sin(angle)
    sine = jnp.where(lane >= HD // 2, -sine, sine)
    for copy in own:
        copy.wait()

    def finish_q(step, _):
        remote(0, step).wait_recv()
        return 0

    def finish_v(step, _):
        remote(1, step).wait_recv()
        return 0

    lax.fori_loop(1, members, finish_q, 0)
    save_q = pltpu.make_async_copy(q_in, gq_ref, load.at[1])
    save_q.start()
    for head in range(H):
        cols = slice(head * HD, (head + 1) * HD)
        x = q_in[:, cols].astype(F32)
        turned[:, cols] = (x * cosine + pltpu.roll(x, HD // 2, 1) * sine).astype(BF16)
    back_q = nt_dot(upq[...], turned[...]).astype(BF16)
    lax.fori_loop(1, members, finish_v, 0)
    save_v = pltpu.make_async_copy(v_in, gv_ref, load.at[2])
    save_v.start()
    back_v = nt_dot(upv[...], v_in[...]).astype(BF16)
    for group in range(groups):
        cols = slice(group * d_cols, (group + 1) * d_cols)
        part[group, 0:8, 0:d_cols] = jnp.dot(back_q, hid[:, cols], preferred_element_type=F32)
        part[group, 8:16, 0:d_cols] = jnp.dot(back_v, hid[:, cols], preferred_element_type=F32)
        cols = slice(group * u_cols, (group + 1) * u_cols)
        part[group, 0:8, d_cols:] = jnp.dot(low_q, turned[:, cols], preferred_element_type=F32)
        part[group, 8:16, d_cols:] = jnp.dot(low_v, v_in[:, cols], preferred_element_type=F32)

    def exchange(step):
        other = across(step)
        return pltpu.make_async_remote_copy(
            src_ref=part.at[other],
            dst_ref=z_in.at[step],
            send_sem=z_send.at[step],
            recv_sem=z_recv.at[step],
            device_id={"dp": other},
            device_id_type=MESH,
        )

    for step in range(1, groups):
        exchange(step).start()
    total = part[dp]
    for step in range(1, groups):
        exchange(step).wait()
        total = total + z_in[step]
    for tile in range(n_tiles):
        column, half = tile // 2, tile % 2
        tiles[tile] = total[half * 8:half * 8 + 8, column * 128:(column + 1) * 128]

    def scatter(step):
        other = partner(me, step)
        return other, pltpu.make_async_remote_copy(
            src_ref=tiles.at[lax.rem(other, n_tiles)],
            dst_ref=r_in.at[step],
            send_sem=r_send.at[step],
            recv_sem=r_recv.at[step],
            device_id={"seq": other},
            device_id_type=MESH,
        )

    def spread(step):
        return pltpu.make_async_remote_copy(
            src_ref=done.at[lax.rem(me, n_tiles)],
            dst_ref=done.at[lax.rem(me, n_tiles)],
            send_sem=a_send.at[step],
            recv_sem=a_recv.at[step],
            device_id={"seq": partner(me, step)},
            device_id_type=MESH,
        )

    def collect(step):
        sender = lax.rem(me + members - step, members)
        return sender, pltpu.make_async_remote_copy(
            src_ref=done.at[lax.rem(sender, n_tiles)],
            dst_ref=done.at[lax.rem(sender, n_tiles)],
            send_sem=a_send.at[step],
            recv_sem=a_recv.at[step],
            device_id={"seq": partner(me, step)},
            device_id_type=MESH,
        )

    def start_scatter(step, _):
        other, copy = scatter(step)

        @pl.when(other < n_tiles)
        def _():
            copy.start()

        return 0

    lax.fori_loop(1, members, start_scatter, 0)

    @pl.when(me < n_tiles)
    def _():
        def wait_scatter(step, _):
            scatter(step)[1].wait_recv()
            return 0

        lax.fori_loop(1, members, wait_scatter, 0)
        summed = tiles[me]
        for step in range(1, members):
            summed = summed + r_in[step]
        done[me] = summed * ADAPTER_SCALE

        def start_spread(step, _):
            spread(step).start()
            return 0

        lax.fori_loop(1, members, start_spread, 0)

    def wait_spread(step, _):
        sender, copy = collect(step)

        @pl.when(sender < n_tiles)
        def _():
            copy.wait_recv()

        return 0

    lax.fori_loop(1, members, wait_spread, 0)
    for column in range(d_tiles):
        cols = slice(column * 128, (column + 1) * 128)
        qd_ref[:, cols] = done[2 * column]
        vd_ref[:, cols] = done[2 * column + 1]
    for column in range(u_tiles):
        cols = slice(column * 128, (column + 1) * 128)
        qu_ref[:, cols] = done[2 * (d_tiles + column)]
        vu_ref[:, cols] = done[2 * (d_tiles + column) + 1]

    def finish(step, _):
        remote(0, step).wait_send()
        remote(1, step).wait_send()
        remote(2, step).wait()
        other, copy = scatter(step)

        @pl.when(other < n_tiles)
        def _():
            copy.wait_send()

        @pl.when(me < n_tiles)
        def _():
            spread(step).wait_send()

        return 0

    lax.fori_loop(1, members, finish, 0)
    save_q.wait()
    save_v.wait()


def adapters(lengths, dq, dk, dv, hidden, down_query, up_query, down_value, up_value):
    rows, model = hidden.shape
    width = up_query.shape[1]
    anywhere = pl.BlockSpec(memory_space=pl.ANY)
    vmem = pl.BlockSpec(memory_space=pltpu.VMEM)
    grad = jax.ShapeDtypeStruct((rows, width), BF16)
    down = jax.ShapeDtypeStruct((RANK, model // 8), F32)
    up = jax.ShapeDtypeStruct((RANK, width // 8), F32)
    each = (model + width) // 8
    n_tiles = 2 * each // 128
    dma = pltpu.SemaphoreType.DMA
    return pl.pallas_call(
        adapter_kernel,
        name="return_and_adapters",
        out_shape=(grad, grad, grad, down, up, down, up),
        in_specs=[pl.BlockSpec(memory_space=pltpu.SMEM)] + [anywhere] * 4 + [vmem] * 4,
        out_specs=[anywhere] * 3 + [vmem] * 4,
        scratch_shapes=[
            pltpu.VMEM((rows, width), BF16),
            pltpu.VMEM((rows, width), BF16),
            pltpu.VMEM((rows, width), BF16),
            pltpu.VMEM((rows, model), BF16),
            pltpu.VMEM((8, 2 * RANK, each), F32),
            pltpu.VMEM((8, 2 * RANK, each), F32),
            pltpu.VMEM((n_tiles, 8, 128), F32),
            pltpu.VMEM((32, 8, 128), F32),
            pltpu.VMEM((n_tiles, 8, 128), F32),
            dma((3, 32)),
            dma((3, 32)),
            dma((3,)),
            dma((3,)),
            dma((8,)),
            dma((8,)),
            dma((32,)),
            dma((32,)),
            dma((32,)),
            dma((32,)),
        ],
        compiler_params=pltpu.CompilerParams(
            collective_id=1, has_side_effects=True, vmem_limit_bytes=32 << 20
        ),
    )(lengths, dq, dk, dv, hidden, down_query, up_query, down_value, up_value)


def shards(
    hidden,
    queries,
    key_states,
    value_states,
    attention_out,
    grad_out,
    lengths,
    down_query,
    up_query,
    down_value,
    up_value,
):
    q, k, v, g, delta = gather_heads(queries, key_states, value_states, grad_out, attention_out)
    dq, dk, dv = attention_backward(lengths, q, k, v, g, delta)
    return adapters(lengths, dq, dk, dv, hidden, down_query, up_query, down_value, up_value)


def solution(mesh):
    tokens = P(("dp", "seq"), None)
    return jax.shard_map(
        shards,
        mesh=mesh,
        in_specs=(tokens,) * 6 + (P("dp", None), P(), P(), P(), P()),
        out_specs=(tokens,) * 3 + (P(None, "dp"),) * 4,
        check_vma=False,
    )
```

```python
import math

import jax
import jax.numpy as jnp
from jax import lax
from jax.experimental import pallas as pl
from jax.experimental.pallas import tpu as pltpu
from jax.sharding import PartitionSpec as P

H = 32
HD = 128
RANK = 8
ADAPTER_SCALE = 2.0
BQ = 512
BK = 512
MESH = pl.DeviceIdType.MESH
NT = (((1,), (1,)), ((), ()))
F32 = jnp.float32
BF16 = jnp.bfloat16


def nt_dot(a, b):
    return lax.dot_general(a, b, NT, preferred_element_type=F32)


def starts_of(len_ref):
    first = len_ref[0, 0]
    second = first + len_ref[0, 1]
    third = second + len_ref[0, 2]
    return first, second, third


def begin_of(positions, starts):
    found = jnp.zeros_like(positions)
    for start in starts:
        found = jnp.where(positions >= start, start, found)
    return found


def partner(me, step):
    chip = lax.rem(lax.rem(step, 16) * 7, 16)
    x = lax.rem(lax.div(me, 8) + lax.div(chip, 4), 4)
    y = lax.rem(lax.div(me, 2) + lax.rem(chip, 4), 4)
    return x * 8 + y * 2 + lax.rem(me + lax.div(step, 16), 2)


def sender_of(me, step):
    chip = lax.rem(lax.rem(step, 16) * 7, 16)
    x = lax.rem(lax.div(me, 8) + 4 - lax.div(chip, 4), 4)
    y = lax.rem(lax.div(me, 2) + 4 - lax.rem(chip, 4), 4)
    return x * 8 + y * 2 + lax.rem(me + lax.div(step, 16), 2)


def gather_kernel(q_ref, k_ref, v_ref, g_ref, o_ref, hq, hk, hv, hg, hd, g_buf, o_buf, d_buf, send, recv, local, load):
    members = 32
    me = lax.axis_index("seq")
    rows = q_ref.shape[0]
    barrier = pltpu.get_barrier_semaphore()

    def greet(step, _):
        pl.semaphore_signal(barrier, inc=1, device_id={"seq": partner(me, step)}, device_id_type=MESH)
        return 0

    lax.fori_loop(1, members, greet, 0)
    load_g = pltpu.make_async_copy(g_ref, g_buf, load.at[0])
    load_o = pltpu.make_async_copy(o_ref, o_buf, load.at[1])
    load_g.start()
    load_o.start()
    pairs = ((q_ref, hq), (k_ref, hk), (v_ref, hv), (g_ref, hg))
    my_rows = pl.ds(pl.multiple_of(me * rows, rows), rows)

    def columns(member):
        return pl.ds(pl.multiple_of(member * HD, HD), HD)

    own = [
        pltpu.make_async_copy(src.at[:, columns(me)], dst.at[my_rows, :], local.at[index])
        for index, (src, dst) in enumerate(pairs)
    ]
    for copy in own:
        copy.start()
    pl.semaphore_wait(barrier, members - 1)

    def remote(index, step):
        src, dst = pairs[index]
        other = partner(me, step)
        return pltpu.make_async_remote_copy(
            src_ref=src.at[:, columns(other)],
            dst_ref=dst.at[my_rows, :],
            send_sem=send.at[index, step],
            recv_sem=recv.at[index, step],
            device_id={"seq": other},
            device_id_type=MESH,
        )

    def remote_delta(step):
        other = partner(me, step)
        return pltpu.make_async_remote_copy(
            src_ref=d_buf.at[other],
            dst_ref=hd.at[me],
            send_sem=send.at[4, step],
            recv_sem=recv.at[4, step],
            device_id={"seq": other},
            device_id_type=MESH,
        )

    def start_all(step, _):
        for index in range(4):
            remote(index, step).start()
        return 0

    lax.fori_loop(1, members, start_all, 0)
    load_g.wait()
    load_o.wait()

    def delta_of(head, _):
        cols = columns(head)
        product = g_buf[:, cols].astype(F32) * o_buf[:, cols].astype(F32)
        d_buf[head] = jnp.sum(product.T, axis=0, keepdims=True)
        return 0

    lax.fori_loop(0, H, delta_of, 0)
    own_delta = pltpu.make_async_copy(d_buf.at[me], hd.at[me], local.at[4])
    own_delta.start()

    def start_delta(step, _):
        remote_delta(step).start()
        return 0

    lax.fori_loop(1, members, start_delta, 0)
    for copy in own:
        copy.wait()
    own_delta.wait()

    def finish(step, _):
        for index in range(4):
            remote(index, step).wait()
        remote_delta(step).wait()
        return 0

    lax.fori_loop(1, members, finish, 0)


def gather_heads(queries, key_states, value_states, grad_out, attention_out):
    rows, width = queries.shape
    hbm = pl.BlockSpec(memory_space=pltpu.HBM)
    vmem = pl.BlockSpec(memory_space=pltpu.VMEM)
    total = rows * 32
    head = jax.ShapeDtypeStruct((total, HD), BF16)
    return pl.pallas_call(
        gather_kernel,
        name="gather_heads",
        out_shape=(head, head, head, head, jax.ShapeDtypeStruct((32, 1, rows), F32)),
        in_specs=[hbm] * 5,
        out_specs=[vmem] * 5,
        scratch_shapes=[
            pltpu.VMEM((rows, width), BF16),
            pltpu.VMEM((rows, width), BF16),
            pltpu.VMEM((H, 1, rows), F32),
            pltpu.SemaphoreType.DMA((5, 32)),
            pltpu.SemaphoreType.DMA((5, 32)),
            pltpu.SemaphoreType.DMA((5,)),
            pltpu.SemaphoreType.DMA((2,)),
        ],
        compiler_params=pltpu.CompilerParams(
            collective_id=0, has_side_effects=True, vmem_limit_bytes=49 << 20
        ),
    )(queries, key_states, value_states, grad_out, attention_out)


def attention_kernel(len_ref, q_ref, k_ref, v_ref, g_ref, d_ref, dq_ref, dk_ref, dv_ref, kt, w_buf, t_buf, dk_acc, dv_acc, stat):
    total = q_ref.shape[0]
    starts = starts_of(len_ref)
    scaling = 1.0 / math.sqrt(HD)
    to_log2 = scaling * math.log2(math.e)
    dk_acc[...] = jnp.zeros_like(dk_acc)
    dv_acc[...] = jnp.zeros_like(dv_acc)

    def turn(block, _):
        at = pl.multiple_of(block * 256, 256)
        kt[:, pl.ds(at, 256)] = k_ref[pl.ds(at, 256), :].T
        return 0

    lax.fori_loop(0, total // 256, turn, 0)

    def fold(x, op):
        return op(x.reshape(x.shape[0] // 8, 8, x.shape[1]), axis=0)

    def outer(query_block, _):
        q0 = pl.multiple_of(query_block * BQ, BQ)
        q_rows = q_ref[pl.ds(q0, BQ), :]
        g_rows = g_ref[pl.ds(q0, BQ), :]
        delta = jnp.concatenate([d_ref[query_block * (BQ // 128) + i] for i in range(BQ // 128)], axis=1)
        query_at = q0 + lax.broadcasted_iota(jnp.int32, (1, BQ), 1)
        query_begin = begin_of(query_at, starts)
        low = begin_of(q0, starts)
        high = begin_of(q0 + (BQ - 1), starts)
        first = lax.div(low, BK)
        last = lax.div(q0 + (BQ - 1), BK) + 1
        stat[0] = jnp.full((8, BQ), -1e30, F32)

        def score(key_block, _):
            k0 = pl.multiple_of(key_block * BK, BK)
            rows = pl.ds(k0, BK)
            inside = jnp.logical_and(high <= k0, k0 + (BK - 1) <= q0)

            @pl.when(inside)
            def _():
                s = nt_dot(k_ref[rows, :], q_rows)
                w_buf[rows, :] = s
                stat[0] = jnp.maximum(stat[0], fold(s, jnp.max))

            @pl.when(jnp.logical_not(inside))
            def _():
                key_at = k0 + lax.broadcasted_iota(jnp.int32, (BK, BQ), 0)
                allowed = jnp.logical_and(key_at >= query_begin, key_at <= query_at)
                s = jnp.where(allowed, nt_dot(k_ref[rows, :], q_rows), -1e30)
                w_buf[rows, :] = s
                stat[0] = jnp.maximum(stat[0], fold(s, jnp.max))

            return 0

        lax.fori_loop(first, last, score, 0)
        top = jnp.max(stat[0], axis=0, keepdims=True)
        stat[1] = jnp.zeros((8, BQ), F32)

        def weigh(key_block, _):
            rows = pl.ds(pl.multiple_of(key_block * BK, BK), BK)
            w = jnp.exp2((w_buf[rows, :] - top) * to_log2)
            stat[1] = stat[1] + fold(w, jnp.sum)
            w_buf[rows, :] = w
            t_buf[rows, :] = w * (nt_dot(v_ref[rows, :], g_rows) - delta)
            return 0

        lax.fori_loop(first, last, weigh, 0)
        inverse = 1.0 / jnp.sum(stat[1], axis=0, keepdims=True)

        def spread(key_block, dq):
            k0 = pl.multiple_of(key_block * BK, BK)
            rows = pl.ds(k0, BK)
            p = (w_buf[rows, :] * inverse).astype(BF16)
            ds = (t_buf[rows, :] * inverse).astype(BF16)
            dv_acc[rows, :] += jnp.dot(p, g_rows, preferred_element_type=F32)
            dk_acc[rows, :] += jnp.dot(ds, q_rows, preferred_element_type=F32)
            return dq + jnp.dot(kt[:, rows], ds, preferred_element_type=F32)

        dq = lax.fori_loop(first, last, spread, jnp.zeros((HD, BQ), F32))
        dq_ref[pl.ds(q0, BQ), :] = (dq * scaling).T.astype(BF16)
        return 0

    lax.fori_loop(0, total // BQ, outer, 0)
    dk_ref[...] = (dk_acc[...] * scaling).astype(BF16)
    dv_ref[...] = dv_acc[...].astype(BF16)


def attention_backward(lengths, q, k, v, g, delta):
    total = q.shape[0]
    vmem = pl.BlockSpec(memory_space=pltpu.VMEM)
    head = jax.ShapeDtypeStruct((total, HD), BF16)
    return pl.pallas_call(
        attention_kernel,
        name="attention_backward",
        out_shape=(head, head, head),
        in_specs=[pl.BlockSpec(memory_space=pltpu.SMEM)] + [vmem] * 5,
        out_specs=[vmem] * 3,
        scratch_shapes=[
            pltpu.VMEM((HD, total), BF16),
            pltpu.VMEM((total, BQ), F32),
            pltpu.VMEM((total, BQ), F32),
            pltpu.VMEM((total, HD), F32),
            pltpu.VMEM((total, HD), F32),
            pltpu.VMEM((2, 8, BQ), F32),
        ],
        compiler_params=pltpu.CompilerParams(vmem_limit_bytes=28 << 20),
    )(lengths, q, k, v, g, delta)


def adapter_kernel(
    len_ref, dq_ref, dk_ref, dv_ref, hid_ref, downq, upq, downv, upv,
    gq_ref, gk_ref, gv_ref, qd_ref, qu_ref, vd_ref, vu_ref,
    turned, hid, part, z_in, tiles, r_in, done,
    send, recv, local, load, z_send, z_recv, r_send, r_recv, a_send, a_recv,
):
    members, groups = 32, 8
    me = lax.axis_index("seq")
    dp = lax.axis_index("dp")
    q_in, v_in = gq_ref, gv_ref
    rows, width = q_in.shape
    model = hid.shape[1]
    d_cols = model // groups
    u_cols = width // groups
    d_tiles = d_cols // 128
    u_tiles = u_cols // 128
    n_tiles = 2 * (d_tiles + u_tiles)
    barrier = pltpu.get_barrier_semaphore()

    def across(step):
        return lax.rem(dp + step, groups)

    def greet(step, _):
        pl.semaphore_signal(barrier, inc=1, device_id={"seq": partner(me, step)}, device_id_type=MESH)
        return 0

    def greet_group(step, _):
        pl.semaphore_signal(barrier, inc=1, device_id={"dp": across(step)}, device_id_type=MESH)
        return 0

    lax.fori_loop(1, members, greet, 0)
    lax.fori_loop(1, groups, greet_group, 0)
    load_hid = pltpu.make_async_copy(hid_ref, hid, load.at[0])
    load_hid.start()
    pairs = ((dq_ref, q_in), (dv_ref, v_in), (dk_ref, gk_ref))
    my_cols = pl.ds(pl.multiple_of(me * HD, HD), HD)

    def rows_of(member):
        return pl.ds(pl.multiple_of(member * rows, rows), rows)

    own = [
        pltpu.make_async_copy(src.at[rows_of(me), :], dst.at[:, my_cols], local.at[index])
        for index, (src, dst) in enumerate(pairs)
    ]
    for copy in own:
        copy.start()
    pl.semaphore_wait(barrier, members - 1 + groups - 1)

    def remote(index, step):
        src, dst = pairs[index]
        other = partner(me, step)
        return pltpu.make_async_remote_copy(
            src_ref=src.at[rows_of(other), :],
            dst_ref=dst.at[:, my_cols],
            send_sem=send.at[index, step],
            recv_sem=recv.at[index, step],
            device_id={"seq": other},
            device_id_type=MESH,
        )

    for index in range(3):
        def start_one(step, _, index=index):
            remote(index, step).start()
            return 0

        lax.fori_loop(1, members, start_one, 0)

    load_hid.wait()
    low_q = nt_dot(downq[...], hid[...]).astype(BF16)
    low_v = nt_dot(downv[...], hid[...]).astype(BF16)
    token = me * rows + lax.broadcasted_iota(jnp.int32, (rows, HD), 0)
    place = (token - begin_of(token, starts_of(len_ref))).astype(F32)
    lane = lax.broadcasted_iota(jnp.int32, (rows, HD), 1)
    pair = jnp.where(lane >= HD // 2, lane - HD // 2, lane).astype(F32)
    angle = place * jnp.exp(-(pair * (2.0 / HD)) * math.log(10000.0))
    cosine = jnp.cos(angle)
    sine = jnp.sin(angle)
    sine = jnp.where(lane >= HD // 2, -sine, sine)
    for copy in own:
        copy.wait()

    def finish_q(step, _):
        remote(0, step).wait_recv()
        return 0

    def finish_v(step, _):
        remote(1, step).wait_recv()
        return 0

    lax.fori_loop(1, members, finish_q, 0)
    for head in range(H):
        cols = slice(head * HD, (head + 1) * HD)
        x = q_in[:, cols].astype(F32)
        turned[:, cols] = (x * cosine + pltpu.roll(x, HD // 2, 1) * sine).astype(BF16)
    back_q = nt_dot(upq[...], turned[...]).astype(BF16)
    lax.fori_loop(1, members, finish_v, 0)
    back_v = nt_dot(upv[...], v_in[...]).astype(BF16)
    for group in range(groups):
        cols = slice(group * d_cols, (group + 1) * d_cols)
        part[group, 0:8, 0:d_cols] = jnp.dot(back_q, hid[:, cols], preferred_element_type=F32)
        part[group, 8:16, 0:d_cols] = jnp.dot(back_v, hid[:, cols], preferred_element_type=F32)
        cols = slice(group * u_cols, (group + 1) * u_cols)
        part[group, 0:8, d_cols:] = jnp.dot(low_q, turned[:, cols], preferred_element_type=F32)
        part[group, 8:16, d_cols:] = jnp.dot(low_v, v_in[:, cols], preferred_element_type=F32)

    def exchange(step):
        other = across(step)
        return pltpu.make_async_remote_copy(
            src_ref=part.at[other],
            dst_ref=z_in.at[step],
            send_sem=z_send.at[step],
            recv_sem=z_recv.at[step],
            device_id={"dp": other},
            device_id_type=MESH,
        )

    for step in range(1, groups):
        exchange(step).start()
    total = part[dp]
    for step in range(1, groups):
        exchange(step).wait()
        total = total + z_in[step]
    for tile in range(n_tiles):
        column, half = tile // 2, tile % 2
        tiles[tile] = total[half * 8:half * 8 + 8, column * 128:(column + 1) * 128]

    def scatter(step):
        other = partner(me, step)
        return other, pltpu.make_async_remote_copy(
            src_ref=tiles.at[lax.rem(other, n_tiles)],
            dst_ref=r_in.at[step],
            send_sem=r_send.at[step],
            recv_sem=r_recv.at[step],
            device_id={"seq": other},
            device_id_type=MESH,
        )

    def spread(step):
        return pltpu.make_async_remote_copy(
            src_ref=done.at[lax.rem(me, n_tiles)],
            dst_ref=done.at[lax.rem(me, n_tiles)],
            send_sem=a_send.at[step],
            recv_sem=a_recv.at[step],
            device_id={"seq": partner(me, step)},
            device_id_type=MESH,
        )

    def collect(step):
        sender = sender_of(me, step)
        return sender, pltpu.make_async_remote_copy(
            src_ref=done.at[lax.rem(sender, n_tiles)],
            dst_ref=done.at[lax.rem(sender, n_tiles)],
            send_sem=a_send.at[step],
            recv_sem=a_recv.at[step],
            device_id={"seq": partner(me, step)},
            device_id_type=MESH,
        )

    def start_scatter(step, _):
        other, copy = scatter(step)

        @pl.when(other < n_tiles)
        def _():
            copy.start()

        return 0

    lax.fori_loop(1, members, start_scatter, 0)

    @pl.when(me < n_tiles)
    def _():
        def wait_scatter(step, _):
            scatter(step)[1].wait_recv()
            return 0

        lax.fori_loop(1, members, wait_scatter, 0)
        summed = tiles[me]
        for step in range(1, members):
            summed = summed + r_in[step]
        done[me] = summed * ADAPTER_SCALE

        def start_spread(step, _):
            spread(step).start()
            return 0

        lax.fori_loop(1, members, start_spread, 0)

    def wait_spread(step, _):
        sender, copy = collect(step)

        @pl.when(sender < n_tiles)
        def _():
            copy.wait_recv()

        return 0

    lax.fori_loop(1, members, wait_spread, 0)
    for column in range(d_tiles):
        cols = slice(column * 128, (column + 1) * 128)
        qd_ref[:, cols] = done[2 * column]
        vd_ref[:, cols] = done[2 * column + 1]
    for column in range(u_tiles):
        cols = slice(column * 128, (column + 1) * 128)
        qu_ref[:, cols] = done[2 * (d_tiles + column)]
        vu_ref[:, cols] = done[2 * (d_tiles + column) + 1]

    def finish(step, _):
        remote(0, step).wait_send()
        remote(1, step).wait_send()
        remote(2, step).wait()
        other, copy = scatter(step)

        @pl.when(other < n_tiles)
        def _():
            copy.wait_send()

        @pl.when(me < n_tiles)
        def _():
            spread(step).wait_send()

        return 0

    lax.fori_loop(1, members, finish, 0)


def adapters(lengths, dq, dk, dv, hidden, down_query, up_query, down_value, up_value):
    rows, model = hidden.shape
    width = up_query.shape[1]
    hbm = pl.BlockSpec(memory_space=pltpu.HBM)
    vmem = pl.BlockSpec(memory_space=pltpu.VMEM)
    grad = jax.ShapeDtypeStruct((rows, width), BF16)
    down = jax.ShapeDtypeStruct((RANK, model // 8), F32)
    up = jax.ShapeDtypeStruct((RANK, width // 8), F32)
    each = (model + width) // 8
    n_tiles = 2 * each // 128
    dma = pltpu.SemaphoreType.DMA
    return pl.pallas_call(
        adapter_kernel,
        name="return_and_adapters",
        out_shape=(grad, grad, grad, down, up, down, up),
        in_specs=[pl.BlockSpec(memory_space=pltpu.SMEM)] + [vmem] * 3 + [hbm] + [vmem] * 4,
        out_specs=[vmem] * 7,
        scratch_shapes=[
            pltpu.VMEM((rows, width), BF16),
            pltpu.VMEM((rows, model), BF16),
            pltpu.VMEM((8, 2 * RANK, each), F32),
            pltpu.VMEM((8, 2 * RANK, each), F32),
            pltpu.VMEM((n_tiles, 8, 128), F32),
            pltpu.VMEM((32, 8, 128), F32),
            pltpu.VMEM((n_tiles, 8, 128), F32),
            dma((3, 32)),
            dma((3, 32)),
            dma((3,)),
            dma((1,)),
            dma((8,)),
            dma((8,)),
            dma((32,)),
            dma((32,)),
            dma((32,)),
            dma((32,)),
        ],
        compiler_params=pltpu.CompilerParams(
            collective_id=1, has_side_effects=True, vmem_limit_bytes=16 << 20
        ),
    )(lengths, dq, dk, dv, hidden, down_query, up_query, down_value, up_value)


def shards(
    hidden,
    queries,
    key_states,
    value_states,
    attention_out,
    grad_out,
    lengths,
    down_query,
    up_query,
    down_value,
    up_value,
):
    q, k, v, g, delta = gather_heads(queries, key_states, value_states, grad_out, attention_out)
    dq, dk, dv = attention_backward(lengths, q, k, v, g, delta)
    return adapters(lengths, dq, dk, dv, hidden, down_query, up_query, down_value, up_value)


def solution(mesh):
    tokens = P(("dp", "seq"), None)
    return jax.shard_map(
        shards,
        mesh=mesh,
        in_specs=(tokens,) * 6 + (P("dp", None), P(), P(), P(), P()),
        out_specs=(tokens,) * 3 + (P(None, "dp"),) * 4,
        check_vma=False,
    )
```

```python
import math

import jax
import jax.numpy as jnp
from jax import lax
from jax.experimental import pallas as pl
from jax.experimental.pallas import tpu as pltpu
from jax.sharding import PartitionSpec as P

H = 32
HD = 128
RANK = 8
ADAPTER_SCALE = 2.0
BQ = 512
BK = 512
GATHER_MIB = 48
LONGEST = 2048
SCALING = 1.0 / math.sqrt(HD)
TO_LOG2 = SCALING * math.log2(math.e)
MESH = pl.DeviceIdType.MESH
NT = (((1,), (1,)), ((), ()))
F32 = jnp.float32
BF16 = jnp.bfloat16


def nt_dot(a, b):
    return lax.dot_general(a, b, NT, preferred_element_type=F32)


def starts_of(len_ref):
    first = len_ref[0, 0]
    second = first + len_ref[0, 1]
    third = second + len_ref[0, 2]
    return first, second, third


def begin_of(positions, starts):
    found = jnp.zeros_like(positions)
    for start in starts:
        found = jnp.where(positions >= start, start, found)
    return found


def partner(me, step):
    chip = lax.rem(lax.rem(step, 16) * 7, 16)
    x = lax.rem(lax.div(me, 8) + lax.div(chip, 4), 4)
    y = lax.rem(lax.div(me, 2) + lax.rem(chip, 4), 4)
    return x * 8 + y * 2 + lax.rem(me + lax.div(step, 16), 2)


def partners(me):
    xs = [lax.rem(lax.div(me, 8) + d, 4) * 8 for d in range(4)]
    ys = [lax.rem(lax.div(me, 2) + d, 4) * 2 for d in range(4)]
    cores = [lax.rem(me + d, 2) for d in range(2)]
    chips = [step % 16 * 7 % 16 for step in range(32)]
    return [xs[chips[step] // 4] + ys[chips[step] % 4] + cores[step // 16] for step in range(32)]


def sender_of(me, step):
    chip = lax.rem(lax.rem(step, 16) * 7, 16)
    x = lax.rem(lax.div(me, 8) + 4 - lax.div(chip, 4), 4)
    y = lax.rem(lax.div(me, 2) + 4 - lax.rem(chip, 4), 4)
    return x * 8 + y * 2 + lax.rem(me + lax.div(step, 16), 2)


def gather_kernel(
    len_ref, q_ref, k_ref, v_ref, g_ref, o_ref, hid_ref, downq, downv,
    hq, hk, hv, hg, hd, hlow, lse, kt, table_ref,
    g_buf, o_buf, hid, wq, wv, d_buf, low, table, stat, send, recv, local, load,
):
    members = 32
    me = lax.axis_index("seq")
    rows = q_ref.shape[0]
    others = partners(me)
    barrier = pltpu.get_barrier_semaphore()
    for step in range(1, members):
        pl.semaphore_signal(barrier, inc=1, device_id={"seq": others[step]}, device_id_type=MESH)
    loads = [
        pltpu.make_async_copy(src, dst, load.at[index])
        for index, (src, dst) in enumerate(
            ((g_ref, g_buf), (o_ref, o_buf), (hid_ref, hid), (downq, wq), (downv, wv))
        )
    ]
    for copy in loads:
        copy.start()
    pairs = ((q_ref, hq), (k_ref, hk), (v_ref, hv), (g_ref, hg))
    my_rows = pl.ds(pl.multiple_of(me * rows, rows), rows)

    def columns(member):
        return pl.ds(pl.multiple_of(member * HD, HD), HD)

    own = [
        pltpu.make_async_copy(src.at[:, columns(me)], dst.at[my_rows, :], local.at[index])
        for index, (src, dst) in enumerate(pairs)
    ]
    for copy in own:
        copy.start()
    pl.semaphore_wait(barrier, members - 1)

    def copies(step, other, indices):
        moves = [(src.at[:, columns(other)], dst.at[my_rows, :]) for src, dst in pairs]
        moves.append((d_buf.at[other], hd.at[me]))
        moves.append((low, hlow.at[:, columns(me)]))
        return [
            pltpu.make_async_remote_copy(
                src_ref=src,
                dst_ref=dst,
                send_sem=send.at[index, step],
                recv_sem=recv.at[index, step],
                device_id={"seq": other},
                device_id_type=MESH,
            )
            for index, (src, dst) in enumerate(moves)
            if index in indices
        ]

    def start(indices):
        for step in range(1, members):
            for copy in copies(step, others[step], indices):
                copy.start()

    start((0, 1))
    for copy in loads:
        copy.wait()

    def delta_of(head, _):
        cols = columns(head)
        product = g_buf[:, cols].astype(F32) * o_buf[:, cols].astype(F32)
        d_buf[head] = jnp.sum(product.T, axis=0, keepdims=True)
        return 0

    lax.fori_loop(0, H, delta_of, 0)
    low[0:8, :] = nt_dot(wq[...], hid[...]).astype(BF16)
    low[8:16, :] = nt_dot(wv[...], hid[...]).astype(BF16)
    own_small = [
        pltpu.make_async_copy(d_buf.at[me], hd.at[me], local.at[4]),
        pltpu.make_async_copy(low, hlow.at[:, columns(me)], local.at[5]),
    ]
    for copy in own_small:
        copy.start()

    start((4, 5))
    start((2, 3))

    starts = starts_of(len_ref)
    lane = lax.broadcasted_iota(jnp.int32, (rows, HD), 1)
    pair = jnp.where(lane >= HD // 2, lane - HD // 2, lane).astype(F32)
    inverse = jnp.exp(-(pair * (2.0 / HD)) * math.log(10000.0))

    def angles(block, _):
        at = pl.multiple_of(block * rows, rows)
        token = at + lax.broadcasted_iota(jnp.int32, (rows, HD), 0)
        angle = (token - begin_of(token, starts)).astype(F32) * inverse
        table[pl.ds(at, rows), :] = jnp.where(lane >= HD // 2, jnp.sin(angle), jnp.cos(angle))
        return 0

    lax.fori_loop(0, members, angles, 0)
    store = pltpu.make_async_copy(table, table_ref, load.at[5])
    store.start()
    for copy in own + own_small:
        copy.wait()

    def arrived(step, _):
        for copy in copies(step, partner(me, step), (0, 1)):
            copy.wait_recv()
        return 0

    lax.fori_loop(1, members, arrived, 0)
    total = hq.shape[0]

    def turn(block, _):
        at = pl.multiple_of(block * 256, 256)
        kt[:, pl.ds(at, 256)] = hk[pl.ds(at, 256), :].T
        return 0

    lax.fori_loop(0, total // 256, turn, 0)

    def statistics(query_block, _):
        q0 = pl.multiple_of(query_block * BQ, BQ)
        q_rows = hq[pl.ds(q0, BQ), :]
        query_at = q0 + lax.broadcasted_iota(jnp.int32, (1, BQ), 1)
        query_begin = begin_of(query_at, starts)
        stat[0] = jnp.full((8, BQ), -1e30, F32)
        stat[1] = jnp.zeros((8, BQ), F32)

        def block(k0, diagonal):
            key_at = k0 + lax.broadcasted_iota(jnp.int32, (BQ, BQ), 0)
            allowed = key_at >= query_begin
            if diagonal:
                allowed = jnp.logical_and(allowed, key_at <= query_at)
            s = jnp.where(allowed, nt_dot(hk[pl.ds(k0, BQ), :], q_rows), -1e30)
            s = s.reshape(BQ // 8, 8, BQ)
            old = stat[0]
            new = jnp.maximum(old, jnp.max(s, axis=0))
            stat[0] = new
            stat[1] = stat[1] * jnp.exp2((old - new) * TO_LOG2) + jnp.sum(jnp.exp2((s - new[None]) * TO_LOG2), axis=0)

        def earlier(key_block, _):
            block(pl.multiple_of(key_block * BQ, BQ), False)
            return 0

        lax.fori_loop(jnp.maximum(query_block - LONGEST // BQ, 0), query_block, earlier, 0)
        block(q0, True)
        top = jnp.max(stat[0], axis=0, keepdims=True)
        weight = jnp.sum(stat[1] * jnp.exp2((stat[0] - top) * TO_LOG2), axis=0, keepdims=True)
        lse[query_block] = top * TO_LOG2 + jnp.log2(weight)
        return 0

    lax.fori_loop(0, total // BQ, statistics, 0)

    def finish(step, _):
        for copy in copies(step, partner(me, step), (0, 1)):
            copy.wait_send()
        for copy in copies(step, partner(me, step), (2, 3, 4, 5)):
            copy.wait()
        return 0

    lax.fori_loop(1, members, finish, 0)
    store.wait()


def gather_heads(lengths, queries, key_states, value_states, grad_out, attention_out, hidden, down_query, down_value):
    rows, width = queries.shape
    model = hidden.shape[1]
    hbm = pl.BlockSpec(memory_space=pltpu.HBM)
    vmem = pl.BlockSpec(memory_space=pltpu.VMEM)
    total = rows * 32
    head = jax.ShapeDtypeStruct((total, HD), BF16)
    return pl.pallas_call(
        gather_kernel,
        name="gather_heads",
        out_shape=(
            head, head, head, head,
            jax.ShapeDtypeStruct((32, 1, rows), F32),
            jax.ShapeDtypeStruct((2 * RANK, total), BF16),
            jax.ShapeDtypeStruct((total // BQ, 1, BQ), F32),
            jax.ShapeDtypeStruct((HD, total), BF16),
            jax.ShapeDtypeStruct((total, HD), F32),
        ),
        in_specs=[pl.BlockSpec(memory_space=pltpu.SMEM)] + [hbm] * 8,
        out_specs=[vmem] * 8 + [hbm],
        scratch_shapes=[
            pltpu.VMEM((rows, width), BF16),
            pltpu.VMEM((rows, width), BF16),
            pltpu.VMEM((rows, model), BF16),
            pltpu.VMEM((RANK, model), BF16),
            pltpu.VMEM((RANK, model), BF16),
            pltpu.VMEM((H, 1, rows), F32),
            pltpu.VMEM((2 * RANK, rows), BF16),
            pltpu.VMEM((total, HD), F32),
            pltpu.VMEM((2, 8, BQ), F32),
            pltpu.SemaphoreType.DMA((6, 32)),
            pltpu.SemaphoreType.DMA((6, 32)),
            pltpu.SemaphoreType.DMA((6,)),
            pltpu.SemaphoreType.DMA((6,)),
        ],
        compiler_params=pltpu.CompilerParams(
            collective_id=0, has_side_effects=True, vmem_limit_bytes=GATHER_MIB << 20
        ),
    )(lengths, queries, key_states, value_states, grad_out, attention_out, hidden, down_query, down_value)


def attention_kernel(
    len_ref, q_ref, k_ref, v_ref, g_ref, d_ref, lse_ref, kt, dq_ref, dk_ref, dv_ref, dk_acc, dv_acc, dq_acc
):
    total = q_ref.shape[0]
    starts = starts_of(len_ref)
    dk_acc[...] = jnp.zeros_like(dk_acc)
    dv_acc[...] = jnp.zeros_like(dv_acc)

    def outer(query_block, _):
        q0 = pl.multiple_of(query_block * BQ, BQ)
        q_rows = q_ref[pl.ds(q0, BQ), :]
        g_rows = g_ref[pl.ds(q0, BQ), :]
        delta = jnp.concatenate([d_ref[query_block * (BQ // 128) + i] for i in range(BQ // 128)], axis=1)
        lse = lse_ref[query_block]
        query_at = q0 + lax.broadcasted_iota(jnp.int32, (1, BQ), 1)
        query_begin = begin_of(query_at, starts)
        low = begin_of(q0, starts)
        high = begin_of(q0 + (BQ - 1), starts)
        first = lax.div(low, BK)
        last = lax.div(q0 + (BQ - 1), BK) + 1
        dq_acc[...] = jnp.zeros_like(dq_acc)

        def pair(key_block, _):
            k0 = pl.multiple_of(key_block * BK, BK)
            rows = pl.ds(k0, BK)
            inside = jnp.logical_and(high <= k0, k0 + (BK - 1) <= q0)

            def spread(s):
                weight = jnp.exp2(s * TO_LOG2 - lse)
                p = weight.astype(BF16)
                ds = (weight * (nt_dot(v_ref[rows, :], g_rows) - delta)).astype(BF16)
                dv_acc[rows, :] += jnp.dot(p, g_rows, preferred_element_type=F32)
                dk_acc[rows, :] += jnp.dot(ds, q_rows, preferred_element_type=F32)
                dq_acc[...] += jnp.dot(kt[:, rows], ds, preferred_element_type=F32)

            @pl.when(inside)
            def _():
                spread(nt_dot(k_ref[rows, :], q_rows))

            @pl.when(jnp.logical_not(inside))
            def _():
                key_at = k0 + lax.broadcasted_iota(jnp.int32, (BK, BQ), 0)
                allowed = jnp.logical_and(key_at >= query_begin, key_at <= query_at)
                spread(jnp.where(allowed, nt_dot(k_ref[rows, :], q_rows), -1e30))

            return 0

        lax.fori_loop(first, last, pair, 0)
        dq_ref[pl.ds(q0, BQ), :] = (dq_acc[...] * SCALING).T.astype(BF16)
        return 0

    lax.fori_loop(0, total // BQ, outer, 0)
    dk_ref[...] = (dk_acc[...] * SCALING).astype(BF16)
    dv_ref[...] = dv_acc[...].astype(BF16)


def attention_backward(lengths, q, k, v, g, delta, lse, kt):
    total = q.shape[0]
    vmem = pl.BlockSpec(memory_space=pltpu.VMEM)
    head = jax.ShapeDtypeStruct((total, HD), BF16)
    return pl.pallas_call(
        attention_kernel,
        name="attention_backward",
        out_shape=(head, head, head),
        in_specs=[pl.BlockSpec(memory_space=pltpu.SMEM)] + [vmem] * 7,
        out_specs=[vmem] * 3,
        scratch_shapes=[
            pltpu.VMEM((total, HD), F32),
            pltpu.VMEM((total, HD), F32),
            pltpu.VMEM((HD, BQ), F32),
        ],
        compiler_params=pltpu.CompilerParams(vmem_limit_bytes=20 << 20),
    )(lengths, q, k, v, g, delta, lse, kt)


def return_kernel(
    dq_ref, dk_ref, dv_ref, table, low, hid, upq, upv,
    gq_ref, gk_ref, gv_ref, done,
    back_out, back_in, part, z_in, up_part, up_in, tiles, r_in,
    send, recv, local, b_send, b_recv, z_send, z_recv, u_send, u_recv, r_send, r_recv, a_send, a_recv, c_send, c_recv,
):
    members, groups = 32, 8
    me = lax.axis_index("seq")
    dp = lax.axis_index("dp")
    rows = gq_ref.shape[0]
    total = dq_ref.shape[0]
    d_cols = hid.shape[1] // groups
    n_tiles = 2 * d_cols // 128
    chunk = 512
    barrier = pltpu.get_barrier_semaphore()

    def across(step):
        return lax.rem(dp + step, groups)

    others = partners(me)
    for step in range(1, members):
        pl.semaphore_signal(barrier, inc=1, device_id={"seq": others[step]}, device_id_type=MESH)
    for step in range(1, groups):
        pl.semaphore_signal(barrier, inc=1, device_id={"dp": across(step)}, device_id_type=MESH)
    pairs = ((dq_ref, gq_ref), (dv_ref, gv_ref), (dk_ref, gk_ref))
    my_cols = pl.ds(pl.multiple_of(me * HD, HD), HD)

    def rows_of(member):
        return pl.ds(pl.multiple_of(member * rows, rows), rows)

    own = [
        pltpu.make_async_copy(src.at[rows_of(me), :], dst.at[:, my_cols], local.at[index])
        for index, (src, dst) in enumerate(pairs)
    ]
    for copy in own:
        copy.start()
    pl.semaphore_wait(barrier, members - 1 + groups - 1)

    def to_member(src, dst, send_sem, recv_sem, other):
        return pltpu.make_async_remote_copy(
            src_ref=src, dst_ref=dst, send_sem=send_sem, recv_sem=recv_sem,
            device_id={"seq": other}, device_id_type=MESH,
        )

    def to_group(src, dst, send_sem, recv_sem, other):
        return pltpu.make_async_remote_copy(
            src_ref=src, dst_ref=dst, send_sem=send_sem, recv_sem=recv_sem,
            device_id={"dp": other}, device_id_type=MESH,
        )

    def bulk(index, step, other):
        src, dst = pairs[index]
        return to_member(
            src.at[rows_of(other), :], dst.at[:, my_cols], send.at[index, step], recv.at[index, step], other
        )

    def start_bulk(index):
        for step in range(1, members):
            bulk(index, step, others[step]).start()

    start_bulk(0)

    up_q = upq[:, my_cols]
    up_v = upv[:, my_cols]

    def share(block, sums):
        sum_q, sum_v = sums
        at = pl.multiple_of(block * chunk, chunk)
        here = pl.ds(at, chunk)
        wave = table[here, :]
        other_half = pltpu.roll(wave, HD // 2, 1)
        first = lax.broadcasted_iota(jnp.int32, (chunk, HD), 1) < HD // 2
        cosine = jnp.where(first, wave, other_half)
        sine = jnp.where(first, other_half, -wave)
        x = dq_ref[here, :].astype(F32)
        pre = (x * cosine + pltpu.roll(x, HD // 2, 1) * sine).astype(BF16)
        value = dv_ref[here, :]
        back_q = nt_dot(up_q, pre)
        back_v = nt_dot(up_v, value)
        for piece in range(chunk // rows):
            cols = slice(piece * rows, (piece + 1) * rows)
            back_out[block * (chunk // rows) + piece, 0:8, :] = back_q[:, cols]
            back_out[block * (chunk // rows) + piece, 8:16, :] = back_v[:, cols]
        low_q = low[0:8, here]
        low_v = low[8:16, here]
        return (
            sum_q + jnp.dot(low_q, pre, preferred_element_type=F32),
            sum_v + jnp.dot(low_v, value, preferred_element_type=F32),
        )

    zero = jnp.zeros((8, HD), F32)
    sum_q, sum_v = lax.fori_loop(0, total // chunk, share, (zero, zero))
    up_part[0] = sum_q
    up_part[1] = sum_v

    def back(step, other):
        return to_member(back_out.at[other], back_in.at[step], b_send.at[step], b_recv.at[step], other)

    for step in range(1, members):
        back(step, others[step]).start()
    owner = lax.div(me, members // groups)
    up_move = to_group(up_part, up_in.at[dp], u_send.at[dp], u_recv.at[dp], owner)

    @pl.when(owner != dp)
    def _():
        up_move.start()

    start_bulk(1)

    def add_back(step, summed):
        back(step, partner(me, step)).wait_recv()
        return summed + back_in[step]

    back_low = lax.fori_loop(1, members, add_back, back_out[me]).astype(BF16)
    for group in range(groups):
        part[group] = jnp.dot(back_low, hid[:, group * d_cols:(group + 1) * d_cols], preferred_element_type=F32)

    def exchange(step):
        other = across(step)
        return to_group(part.at[other], z_in.at[step], z_send.at[step], z_recv.at[step], other)

    for step in range(1, groups):
        exchange(step).start()
    start_bulk(2)

    def place_of(member):
        return pl.ds(n_tiles + 2 * lax.rem(member, members // groups), 2)

    def spread_up(step, other):
        mine = done.at[place_of(me)]
        return to_member(mine, mine, c_send.at[step], c_recv.at[step], other)

    def collect_up(step):
        theirs = done.at[place_of(sender_of(me, step))]
        return to_member(theirs, theirs, c_send.at[step], c_recv.at[step], partner(me, step))

    @pl.when(owner == dp)
    def _():
        summed = up_part[...]
        for step in range(1, groups):
            source = across(step)
            to_group(up_part, up_in.at[source], u_send.at[source], u_recv.at[source], source).wait_recv()
            summed = summed + up_in[source]
        done[place_of(me)] = summed * ADAPTER_SCALE

        for step in range(1, members):
            spread_up(step, others[step]).start()

    down = part[dp]
    for step in range(1, groups):
        exchange(step).wait()
        down = down + z_in[step]
    for tile in range(n_tiles):
        column, half = tile // 2, tile % 2
        tiles[tile] = down[half * 8:half * 8 + 8, column * 128:(column + 1) * 128]

    def scatter(step, other):
        return to_member(
            tiles.at[lax.rem(other, n_tiles)], r_in.at[step], r_send.at[step], r_recv.at[step], other
        )

    def spread(step, other):
        mine = done.at[lax.rem(me, n_tiles)]
        return to_member(mine, mine, a_send.at[step], a_recv.at[step], other)

    def collect(step):
        sender = sender_of(me, step)
        theirs = done.at[lax.rem(sender, n_tiles)]
        return sender, to_member(theirs, theirs, a_send.at[step], a_recv.at[step], partner(me, step))

    for step in range(1, members):
        @pl.when(others[step] < n_tiles)
        def _(step=step):
            scatter(step, others[step]).start()

    @pl.when(me < n_tiles)
    def _():
        def add_tile(step, summed):
            scatter(step, partner(me, step)).wait_recv()
            return summed + r_in[step]

        done[me] = lax.fori_loop(1, members, add_tile, tiles[me]) * ADAPTER_SCALE

        for step in range(1, members):
            spread(step, others[step]).start()

    def finish(step, _):
        for index in range(3):
            bulk(index, step, partner(me, step)).wait()
        back(step, partner(me, step)).wait_send()
        other = partner(me, step)

        @pl.when(other < n_tiles)
        def _():
            scatter(step, other).wait_send()

        @pl.when(me < n_tiles)
        def _():
            spread(step, other).wait_send()

        @pl.when(owner == dp)
        def _():
            spread_up(step, other).wait_send()

        sender, piece = collect(step)

        @pl.when(sender < n_tiles)
        def _():
            piece.wait_recv()

        @pl.when(lax.div(sender, members // groups) == dp)
        def _():
            collect_up(step).wait_recv()

        return 0

    lax.fori_loop(1, members, finish, 0)

    @pl.when(owner != dp)
    def _():
        up_move.wait_send()

    for copy in own:
        copy.wait()


def return_heads(dq, dk, dv, table, low, hidden, up_query, up_value):
    rows, model = hidden.shape
    total = dq.shape[0]
    width = up_query.shape[1]
    vmem = pl.BlockSpec(memory_space=pltpu.VMEM)
    grad = jax.ShapeDtypeStruct((rows, width), BF16)
    d_cols = model // 8
    n_tiles = 2 * d_cols // 128
    all_tiles = n_tiles + 2 * (width // 8) // 128
    dma = pltpu.SemaphoreType.DMA
    return pl.pallas_call(
        return_kernel,
        name="return_heads",
        out_shape=(grad, grad, grad, jax.ShapeDtypeStruct((all_tiles, 8, 128), F32)),
        in_specs=[vmem] * 8,
        out_specs=[vmem] * 4,
        scratch_shapes=[
            pltpu.VMEM((32, 2 * RANK, rows), F32),
            pltpu.VMEM((32, 2 * RANK, rows), F32),
            pltpu.VMEM((8, 2 * RANK, d_cols), F32),
            pltpu.VMEM((8, 2 * RANK, d_cols), F32),
            pltpu.VMEM((2, RANK, HD), F32),
            pltpu.VMEM((8, 2, RANK, HD), F32),
            pltpu.VMEM((n_tiles, 8, 128), F32),
            pltpu.VMEM((32, 8, 128), F32),
            dma((3, 32)), dma((3, 32)), dma((3,)),
            dma((32,)), dma((32,)),
            dma((8,)), dma((8,)),
            dma((8,)), dma((8,)),
            dma((32,)), dma((32,)),
            dma((32,)), dma((32,)),
            dma((32,)), dma((32,)),
        ],
        compiler_params=pltpu.CompilerParams(
            collective_id=1, has_side_effects=True, vmem_limit_bytes=16 << 20
        ),
    )(dq, dk, dv, table, low, hidden, up_query, up_value)


def finish_kernel(gq, gk, gv, done, oq, ok, ov, qd, qu, vd, vu, sems):
    copies = [
        pltpu.make_async_copy(src, dst, sems.at[index])
        for index, (src, dst) in enumerate(((gq, oq), (gk, ok), (gv, ov)))
    ]
    for copy in copies:
        copy.start()
    d_tiles = qd.shape[1] // 128
    for column in range(d_tiles):
        cols = slice(column * 128, (column + 1) * 128)
        qd[:, cols] = done[2 * column]
        vd[:, cols] = done[2 * column + 1]
    for column in range(qu.shape[1] // 128):
        cols = slice(column * 128, (column + 1) * 128)
        qu[:, cols] = done[2 * (d_tiles + column)]
        vu[:, cols] = done[2 * (d_tiles + column) + 1]
    for copy in copies:
        copy.wait()


def write_results(gq, gk, gv, done, model):
    rows, width = gq.shape
    vmem = pl.BlockSpec(memory_space=pltpu.VMEM)
    hbm = pl.BlockSpec(memory_space=pltpu.HBM)
    grad = jax.ShapeDtypeStruct((rows, width), BF16)
    down = jax.ShapeDtypeStruct((RANK, model // 8), F32)
    up = jax.ShapeDtypeStruct((RANK, width // 8), F32)
    return pl.pallas_call(
        finish_kernel,
        name="write_results",
        out_shape=(grad, grad, grad, down, up, down, up),
        in_specs=[vmem] * 4,
        out_specs=[hbm] * 3 + [vmem] * 4,
        scratch_shapes=[pltpu.SemaphoreType.DMA((3,))],
        compiler_params=pltpu.CompilerParams(vmem_limit_bytes=4 << 20),
    )(gq, gk, gv, done)


def shards(
    hidden,
    queries,
    key_states,
    value_states,
    attention_out,
    grad_out,
    lengths,
    down_query,
    up_query,
    down_value,
    up_value,
):
    q, k, v, g, delta, low, lse, kt, table = gather_heads(
        lengths, queries, key_states, value_states, grad_out, attention_out, hidden, down_query, down_value
    )
    dq, dk, dv = attention_backward(lengths, q, k, v, g, delta, lse, kt)
    gq, gk, gv, done = return_heads(dq, dk, dv, table, low, hidden, up_query, up_value)
    return write_results(gq, gk, gv, done, hidden.shape[1])


def solution(mesh):
    tokens = P(("dp", "seq"), None)
    return jax.shard_map(
        shards,
        mesh=mesh,
        in_specs=(tokens,) * 6 + (P("dp", None), P(), P(), P(), P()),
        out_specs=(tokens,) * 3 + (P(None, "dp"),) * 4,
        check_vma=False,
    )
```

```python
import math

import jax
import jax.numpy as jnp
from jax import lax
from jax.experimental import pallas as pl
from jax.experimental.pallas import tpu as pltpu
from jax.sharding import PartitionSpec as P

H = 32
HD = 128
RANK = 8
ADAPTER_SCALE = 2.0
BQ = 512
BK = 512
GATHER_MIB = 48
LONGEST = 2048
SCALING = 1.0 / math.sqrt(HD)
TO_LOG2 = SCALING * math.log2(math.e)
MESH = pl.DeviceIdType.MESH
NT = (((1,), (1,)), ((), ()))
F32 = jnp.float32
BF16 = jnp.bfloat16


def nt_dot(a, b):
    return lax.dot_general(a, b, NT, preferred_element_type=F32)


def starts_of(len_ref):
    first = len_ref[0, 0]
    second = first + len_ref[0, 1]
    third = second + len_ref[0, 2]
    return first, second, third


def begin_of(positions, starts):
    found = jnp.zeros_like(positions)
    for start in starts:
        found = jnp.where(positions >= start, start, found)
    return found


def partner(me, step):
    chip = lax.rem(lax.rem(step, 16) * 7, 16)
    x = lax.rem(lax.div(me, 8) + lax.div(chip, 4), 4)
    y = lax.rem(lax.div(me, 2) + lax.rem(chip, 4), 4)
    return x * 8 + y * 2 + lax.rem(me + lax.div(step, 16), 2)


def partners(me):
    xs = [lax.rem(lax.div(me, 8) + d, 4) * 8 for d in range(4)]
    ys = [lax.rem(lax.div(me, 2) + d, 4) * 2 for d in range(4)]
    cores = [lax.rem(me + d, 2) for d in range(2)]
    chips = [step % 16 * 7 % 16 for step in range(32)]
    return [xs[chips[step] // 4] + ys[chips[step] % 4] + cores[step // 16] for step in range(32)]


def sender_of(me, step):
    chip = lax.rem(lax.rem(step, 16) * 7, 16)
    x = lax.rem(lax.div(me, 8) + 4 - lax.div(chip, 4), 4)
    y = lax.rem(lax.div(me, 2) + 4 - lax.rem(chip, 4), 4)
    return x * 8 + y * 2 + lax.rem(me + lax.div(step, 16), 2)


def gather_kernel(
    len_ref, q_ref, k_ref, v_ref, g_ref, o_ref, hid_ref, downq, downv,
    hq, hk, hv, hg, hd, hlow, lse, kt, table_ref,
    g_buf, o_buf, hid, wq, wv, d_buf, low, table, stat, send, recv, local, load,
):
    members = 32
    me = lax.axis_index("seq")
    rows = q_ref.shape[0]
    others = partners(me)
    barrier = pltpu.get_barrier_semaphore()
    for step in range(1, members):
        pl.semaphore_signal(barrier, inc=1, device_id={"seq": others[step]}, device_id_type=MESH)
    loads = [
        pltpu.make_async_copy(src, dst, load.at[index])
        for index, (src, dst) in enumerate(
            ((g_ref, g_buf), (o_ref, o_buf), (hid_ref, hid), (downq, wq), (downv, wv))
        )
    ]
    for copy in loads:
        copy.start()
    pairs = ((q_ref, hq), (k_ref, hk), (v_ref, hv), (g_ref, hg))
    my_rows = pl.ds(pl.multiple_of(me * rows, rows), rows)

    def columns(member):
        return pl.ds(pl.multiple_of(member * HD, HD), HD)

    own = [
        pltpu.make_async_copy(src.at[:, columns(me)], dst.at[my_rows, :], local.at[index])
        for index, (src, dst) in enumerate(pairs)
    ]
    for copy in own:
        copy.start()
    pl.semaphore_wait(barrier, members - 1)

    def copies(step, other, indices):
        moves = [(src.at[:, columns(other)], dst.at[my_rows, :]) for src, dst in pairs]
        moves.append((d_buf.at[other], hd.at[me]))
        moves.append((low, hlow.at[:, columns(me)]))
        return [
            pltpu.make_async_remote_copy(
                src_ref=src,
                dst_ref=dst,
                send_sem=send.at[index, step],
                recv_sem=recv.at[index, step],
                device_id={"seq": other},
                device_id_type=MESH,
            )
            for index, (src, dst) in enumerate(moves)
            if index in indices
        ]

    def start(indices):
        for step in range(1, members):
            for copy in copies(step, others[step], indices):
                copy.start()

    start((0, 1))
    for copy in loads:
        copy.wait()

    def delta_of(head, _):
        cols = columns(head)
        product = g_buf[:, cols].astype(F32) * o_buf[:, cols].astype(F32)
        d_buf[head] = jnp.sum(product.T, axis=0, keepdims=True)
        return 0

    lax.fori_loop(0, H, delta_of, 0)
    low[0:8, :] = nt_dot(wq[...], hid[...]).astype(BF16)
    low[8:16, :] = nt_dot(wv[...], hid[...]).astype(BF16)
    own_small = [
        pltpu.make_async_copy(d_buf.at[me], hd.at[me], local.at[4]),
        pltpu.make_async_copy(low, hlow.at[:, columns(me)], local.at[5]),
    ]
    for copy in own_small:
        copy.start()

    start((4, 5))
    start((2, 3))

    starts = starts_of(len_ref)
    lane = lax.broadcasted_iota(jnp.int32, (rows, HD), 1)
    pair = jnp.where(lane >= HD // 2, lane - HD // 2, lane).astype(F32)
    inverse = jnp.exp(-(pair * (2.0 / HD)) * math.log(10000.0))

    def angles(block, _):
        at = pl.multiple_of(block * rows, rows)
        token = at + lax.broadcasted_iota(jnp.int32, (rows, HD), 0)
        angle = (token - begin_of(token, starts)).astype(F32) * inverse
        table[pl.ds(at, rows), :] = jnp.where(lane >= HD // 2, jnp.sin(angle), jnp.cos(angle))
        return 0

    lax.fori_loop(0, members, angles, 0)
    store = pltpu.make_async_copy(table, table_ref, load.at[5])
    store.start()
    for copy in own + own_small:
        copy.wait()

    def arrived(step, _):
        for copy in copies(step, partner(me, step), (0, 1)):
            copy.wait_recv()
        return 0

    lax.fori_loop(1, members, arrived, 0)
    total = hq.shape[0]

    def turn(block, _):
        at = pl.multiple_of(block * 256, 256)
        kt[:, pl.ds(at, 256)] = hk[pl.ds(at, 256), :].T
        return 0

    lax.fori_loop(0, total // 256, turn, 0)

    def statistics(query_block, _):
        q0 = pl.multiple_of(query_block * BQ, BQ)
        q_rows = hq[pl.ds(q0, BQ), :]
        query_at = q0 + lax.broadcasted_iota(jnp.int32, (1, BQ), 1)
        query_begin = begin_of(query_at, starts)
        stat[0] = jnp.full((8, BQ), -1e30, F32)
        stat[1] = jnp.zeros((8, BQ), F32)

        def block(k0, diagonal):
            key_at = k0 + lax.broadcasted_iota(jnp.int32, (BQ, BQ), 0)
            allowed = key_at >= query_begin
            if diagonal:
                allowed = jnp.logical_and(allowed, key_at <= query_at)
            s = jnp.where(allowed, nt_dot(hk[pl.ds(k0, BQ), :], q_rows), -1e30)
            s = s.reshape(BQ // 8, 8, BQ)
            old = stat[0]
            new = jnp.maximum(old, jnp.max(s, axis=0))
            stat[0] = new
            stat[1] = stat[1] * jnp.exp2((old - new) * TO_LOG2) + jnp.sum(jnp.exp2((s - new[None]) * TO_LOG2), axis=0)

        def earlier(key_block, _):
            block(pl.multiple_of(key_block * BQ, BQ), False)
            return 0

        lax.fori_loop(jnp.maximum(query_block - LONGEST // BQ, 0), query_block, earlier, 0)
        block(q0, True)
        top = jnp.max(stat[0], axis=0, keepdims=True)
        weight = jnp.sum(stat[1] * jnp.exp2((stat[0] - top) * TO_LOG2), axis=0, keepdims=True)
        lse[query_block] = top * TO_LOG2 + jnp.log2(weight)
        return 0

    lax.fori_loop(0, total // BQ, statistics, 0)

    def finish(step, _):
        for copy in copies(step, partner(me, step), (0, 1)):
            copy.wait_send()
        for copy in copies(step, partner(me, step), (2, 3, 4, 5)):
            copy.wait()
        return 0

    lax.fori_loop(1, members, finish, 0)
    store.wait()


def gather_heads(lengths, queries, key_states, value_states, grad_out, attention_out, hidden, down_query, down_value):
    rows, width = queries.shape
    model = hidden.shape[1]
    hbm = pl.BlockSpec(memory_space=pltpu.HBM)
    vmem = pl.BlockSpec(memory_space=pltpu.VMEM)
    total = rows * 32
    head = jax.ShapeDtypeStruct((total, HD), BF16)
    return pl.pallas_call(
        gather_kernel,
        name="gather_heads",
        out_shape=(
            head, head, head, head,
            jax.ShapeDtypeStruct((32, 1, rows), F32),
            jax.ShapeDtypeStruct((2 * RANK, total), BF16),
            jax.ShapeDtypeStruct((total // BQ, 1, BQ), F32),
            jax.ShapeDtypeStruct((HD, total), BF16),
            jax.ShapeDtypeStruct((total, HD), F32),
        ),
        in_specs=[pl.BlockSpec(memory_space=pltpu.SMEM)] + [hbm] * 8,
        out_specs=[vmem] * 8 + [hbm],
        scratch_shapes=[
            pltpu.VMEM((rows, width), BF16),
            pltpu.VMEM((rows, width), BF16),
            pltpu.VMEM((rows, model), BF16),
            pltpu.VMEM((RANK, model), BF16),
            pltpu.VMEM((RANK, model), BF16),
            pltpu.VMEM((H, 1, rows), F32),
            pltpu.VMEM((2 * RANK, rows), BF16),
            pltpu.VMEM((total, HD), F32),
            pltpu.VMEM((2, 8, BQ), F32),
            pltpu.SemaphoreType.DMA((6, 32)),
            pltpu.SemaphoreType.DMA((6, 32)),
            pltpu.SemaphoreType.DMA((6,)),
            pltpu.SemaphoreType.DMA((6,)),
        ],
        compiler_params=pltpu.CompilerParams(
            collective_id=0, has_side_effects=True, vmem_limit_bytes=GATHER_MIB << 20
        ),
    )(lengths, queries, key_states, value_states, grad_out, attention_out, hidden, down_query, down_value)


def attention_kernel(
    len_ref, q_ref, k_ref, v_ref, g_ref, d_ref, lse_ref, kt, dq_ref, dk_ref, dv_ref, dk_acc, dv_acc, dq_acc
):
    total = q_ref.shape[0]
    starts = starts_of(len_ref)
    dk_acc[...] = jnp.zeros_like(dk_acc)
    dv_acc[...] = jnp.zeros_like(dv_acc)

    def outer(query_block, _):
        q0 = pl.multiple_of(query_block * BQ, BQ)
        q_rows = q_ref[pl.ds(q0, BQ), :]
        g_rows = g_ref[pl.ds(q0, BQ), :]
        delta = jnp.concatenate([d_ref[query_block * (BQ // 128) + i] for i in range(BQ // 128)], axis=1)
        lse = lse_ref[query_block]
        query_at = q0 + lax.broadcasted_iota(jnp.int32, (1, BQ), 1)
        query_begin = begin_of(query_at, starts)
        low = begin_of(q0, starts)
        high = begin_of(q0 + (BQ - 1), starts)
        first = lax.div(low, BK)
        last = lax.div(q0 + (BQ - 1), BK) + 1
        dq_acc[...] = jnp.zeros_like(dq_acc)

        def pair(key_block, _):
            k0 = pl.multiple_of(key_block * BK, BK)
            rows = pl.ds(k0, BK)
            inside = jnp.logical_and(high <= k0, k0 + (BK - 1) <= q0)

            def spread(s):
                weight = jnp.exp2(s * TO_LOG2 - lse)
                p = weight.astype(BF16)
                ds = (weight * (nt_dot(v_ref[rows, :], g_rows) - delta)).astype(BF16)
                dv_acc[rows, :] += jnp.dot(p, g_rows, preferred_element_type=F32)
                dk_acc[rows, :] += jnp.dot(ds, q_rows, preferred_element_type=F32)
                dq_acc[...] += jnp.dot(kt[:, rows], ds, preferred_element_type=F32)

            @pl.when(inside)
            def _():
                spread(nt_dot(k_ref[rows, :], q_rows))

            @pl.when(jnp.logical_not(inside))
            def _():
                key_at = k0 + lax.broadcasted_iota(jnp.int32, (BK, BQ), 0)
                allowed = jnp.logical_and(key_at >= query_begin, key_at <= query_at)
                spread(jnp.where(allowed, nt_dot(k_ref[rows, :], q_rows), -1e30))

            return 0

        lax.fori_loop(first, last, pair, 0)
        dq_ref[pl.ds(q0, BQ), :] = (dq_acc[...] * SCALING).T.astype(BF16)
        return 0

    lax.fori_loop(0, total // BQ, outer, 0)
    dk_ref[...] = (dk_acc[...] * SCALING).astype(BF16)
    dv_ref[...] = dv_acc[...].astype(BF16)


def attention_backward(lengths, q, k, v, g, delta, lse, kt):
    total = q.shape[0]
    vmem = pl.BlockSpec(memory_space=pltpu.VMEM)
    head = jax.ShapeDtypeStruct((total, HD), BF16)
    return pl.pallas_call(
        attention_kernel,
        name="attention_backward",
        out_shape=(head, head, head),
        in_specs=[pl.BlockSpec(memory_space=pltpu.SMEM)] + [vmem] * 7,
        out_specs=[vmem] * 3,
        scratch_shapes=[
            pltpu.VMEM((total, HD), F32),
            pltpu.VMEM((total, HD), F32),
            pltpu.VMEM((HD, BQ), F32),
        ],
        compiler_params=pltpu.CompilerParams(vmem_limit_bytes=20 << 20),
    )(lengths, q, k, v, g, delta, lse, kt)


def return_kernel(
    dq_ref, dk_ref, dv_ref, table, low, hid, upq, upv,
    gq_ref, gk_ref, gv_ref, done,
    back_out, back_in, part, z_in, up_part, up_in, tiles, r_in,
    send, recv, local, b_send, b_recv, z_send, z_recv, u_send, u_recv, r_send, r_recv, a_send, a_recv, c_send, c_recv,
):
    members, groups = 32, 8
    me = lax.axis_index("seq")
    dp = lax.axis_index("dp")
    rows = gq_ref.shape[0]
    total = dq_ref.shape[0]
    d_cols = hid.shape[1] // groups
    n_tiles = 2 * d_cols // 128
    chunk = 512
    barrier = pltpu.get_barrier_semaphore()

    def across(step):
        return lax.rem(dp + step, groups)

    others = partners(me)
    for step in range(1, members):
        pl.semaphore_signal(barrier, inc=1, device_id={"seq": others[step]}, device_id_type=MESH)
    for step in range(1, groups):
        pl.semaphore_signal(barrier, inc=1, device_id={"dp": across(step)}, device_id_type=MESH)
    pairs = ((dq_ref, gq_ref), (dv_ref, gv_ref), (dk_ref, gk_ref))
    my_cols = pl.ds(pl.multiple_of(me * HD, HD), HD)

    def rows_of(member):
        return pl.ds(pl.multiple_of(member * rows, rows), rows)

    own = [
        pltpu.make_async_copy(src.at[rows_of(me), :], dst.at[:, my_cols], local.at[index])
        for index, (src, dst) in enumerate(pairs)
    ]
    for copy in own:
        copy.start()
    pl.semaphore_wait(barrier, members - 1 + groups - 1)

    def to_member(src, dst, send_sem, recv_sem, other):
        return pltpu.make_async_remote_copy(
            src_ref=src, dst_ref=dst, send_sem=send_sem, recv_sem=recv_sem,
            device_id={"seq": other}, device_id_type=MESH,
        )

    def to_group(src, dst, send_sem, recv_sem, other):
        return pltpu.make_async_remote_copy(
            src_ref=src, dst_ref=dst, send_sem=send_sem, recv_sem=recv_sem,
            device_id={"dp": other}, device_id_type=MESH,
        )

    def bulk(index, step, other):
        src, dst = pairs[index]
        return to_member(
            src.at[rows_of(other), :], dst.at[:, my_cols], send.at[index, step], recv.at[index, step], other
        )

    near = range(1, members // 2)
    far = range(members // 2, members)

    def start_bulk(index, steps):
        for step in steps:
            bulk(index, step, others[step]).start()

    start_bulk(0, near)

    up_q = upq[:, my_cols]
    up_v = upv[:, my_cols]

    def share(block, sums):
        sum_q, sum_v = sums
        at = pl.multiple_of(block * chunk, chunk)
        here = pl.ds(at, chunk)
        wave = table[here, :]
        other_half = pltpu.roll(wave, HD // 2, 1)
        first = lax.broadcasted_iota(jnp.int32, (chunk, HD), 1) < HD // 2
        cosine = jnp.where(first, wave, other_half)
        sine = jnp.where(first, other_half, -wave)
        x = dq_ref[here, :].astype(F32)
        pre = (x * cosine + pltpu.roll(x, HD // 2, 1) * sine).astype(BF16)
        value = dv_ref[here, :]
        back_q = nt_dot(up_q, pre)
        back_v = nt_dot(up_v, value)
        for piece in range(chunk // rows):
            cols = slice(piece * rows, (piece + 1) * rows)
            back_out[block * (chunk // rows) + piece, 0:8, :] = back_q[:, cols]
            back_out[block * (chunk // rows) + piece, 8:16, :] = back_v[:, cols]
        low_q = low[0:8, here]
        low_v = low[8:16, here]
        return (
            sum_q + jnp.dot(low_q, pre, preferred_element_type=F32),
            sum_v + jnp.dot(low_v, value, preferred_element_type=F32),
        )

    zero = jnp.zeros((8, HD), F32)
    sum_q, sum_v = lax.fori_loop(0, total // chunk, share, (zero, zero))
    up_part[0] = sum_q
    up_part[1] = sum_v

    def back(step, other):
        return to_member(back_out.at[other], back_in.at[step], b_send.at[step], b_recv.at[step], other)

    for step in range(1, members):
        back(step, others[step]).start()
    owner = lax.div(me, members // groups)
    up_move = to_group(up_part, up_in.at[dp], u_send.at[dp], u_recv.at[dp], owner)

    @pl.when(owner != dp)
    def _():
        up_move.start()

    start_bulk(0, far)

    def add_back(step, summed):
        back(step, partner(me, step)).wait_recv()
        return summed + back_in[step]

    back_low = lax.fori_loop(1, members, add_back, back_out[me]).astype(BF16)

    def fill(group):
        cols = pl.ds(pl.multiple_of(group * d_cols, 128), d_cols)
        part[group] = jnp.dot(back_low, hid[:, cols], preferred_element_type=F32)

    def exchange(step):
        other = across(step)
        return to_group(part.at[other], z_in.at[step], z_send.at[step], z_recv.at[step], other)

    for step in range(1, groups):
        fill(across(step))
        exchange(step).start()
    start_bulk(1, near)
    start_bulk(1, far)
    fill(dp)

    def place_of(member):
        return pl.ds(n_tiles + 2 * lax.rem(member, members // groups), 2)

    def spread_up(step, other):
        mine = done.at[place_of(me)]
        return to_member(mine, mine, c_send.at[step], c_recv.at[step], other)

    def collect_up(step):
        theirs = done.at[place_of(sender_of(me, step))]
        return to_member(theirs, theirs, c_send.at[step], c_recv.at[step], partner(me, step))

    @pl.when(owner == dp)
    def _():
        summed = up_part[...]
        for step in range(1, groups):
            source = across(step)
            to_group(up_part, up_in.at[source], u_send.at[source], u_recv.at[source], source).wait_recv()
            summed = summed + up_in[source]
        done[place_of(me)] = summed * ADAPTER_SCALE

        for step in range(1, members):
            spread_up(step, others[step]).start()

    down = part[dp]
    for step in range(1, groups):
        exchange(step).wait()
        down = down + z_in[step]
    for tile in range(n_tiles):
        column, half = tile // 2, tile % 2
        tiles[tile] = down[half * 8:half * 8 + 8, column * 128:(column + 1) * 128]

    def scatter(step, other):
        return to_member(
            tiles.at[lax.rem(other, n_tiles)], r_in.at[step], r_send.at[step], r_recv.at[step], other
        )

    def spread(step, other):
        mine = done.at[lax.rem(me, n_tiles)]
        return to_member(mine, mine, a_send.at[step], a_recv.at[step], other)

    def collect(step):
        sender = sender_of(me, step)
        theirs = done.at[lax.rem(sender, n_tiles)]
        return sender, to_member(theirs, theirs, a_send.at[step], a_recv.at[step], partner(me, step))

    for step in range(1, members):
        @pl.when(others[step] < n_tiles)
        def _(step=step):
            scatter(step, others[step]).start()

    start_bulk(2, near)

    @pl.when(me < n_tiles)
    def _():
        def add_tile(step, summed):
            scatter(step, partner(me, step)).wait_recv()
            return summed + r_in[step]

        done[me] = lax.fori_loop(1, members, add_tile, tiles[me]) * ADAPTER_SCALE

        for step in range(1, members):
            spread(step, others[step]).start()

    start_bulk(2, far)

    def finish(step, _):
        for index in range(3):
            bulk(index, step, partner(me, step)).wait()
        back(step, partner(me, step)).wait_send()
        other = partner(me, step)

        @pl.when(other < n_tiles)
        def _():
            scatter(step, other).wait_send()

        @pl.when(me < n_tiles)
        def _():
            spread(step, other).wait_send()

        @pl.when(owner == dp)
        def _():
            spread_up(step, other).wait_send()

        sender, piece = collect(step)

        @pl.when(sender < n_tiles)
        def _():
            piece.wait_recv()

        @pl.when(lax.div(sender, members // groups) == dp)
        def _():
            collect_up(step).wait_recv()

        return 0

    lax.fori_loop(1, members, finish, 0)

    @pl.when(owner != dp)
    def _():
        up_move.wait_send()

    for copy in own:
        copy.wait()


def return_heads(dq, dk, dv, table, low, hidden, up_query, up_value):
    rows, model = hidden.shape
    total = dq.shape[0]
    width = up_query.shape[1]
    vmem = pl.BlockSpec(memory_space=pltpu.VMEM)
    grad = jax.ShapeDtypeStruct((rows, width), BF16)
    d_cols = model // 8
    n_tiles = 2 * d_cols // 128
    all_tiles = n_tiles + 2 * (width // 8) // 128
    dma = pltpu.SemaphoreType.DMA
    return pl.pallas_call(
        return_kernel,
        name="return_heads",
        out_shape=(grad, grad, grad, jax.ShapeDtypeStruct((all_tiles, 8, 128), F32)),
        in_specs=[vmem] * 8,
        out_specs=[vmem] * 4,
        scratch_shapes=[
            pltpu.VMEM((32, 2 * RANK, rows), F32),
            pltpu.VMEM((32, 2 * RANK, rows), F32),
            pltpu.VMEM((8, 2 * RANK, d_cols), F32),
            pltpu.VMEM((8, 2 * RANK, d_cols), F32),
            pltpu.VMEM((2, RANK, HD), F32),
            pltpu.VMEM((8, 2, RANK, HD), F32),
            pltpu.VMEM((n_tiles, 8, 128), F32),
            pltpu.VMEM((32, 8, 128), F32),
            dma((3, 32)), dma((3, 32)), dma((3,)),
            dma((32,)), dma((32,)),
            dma((8,)), dma((8,)),
            dma((8,)), dma((8,)),
            dma((32,)), dma((32,)),
            dma((32,)), dma((32,)),
            dma((32,)), dma((32,)),
        ],
        compiler_params=pltpu.CompilerParams(
            collective_id=1, has_side_effects=True, vmem_limit_bytes=16 << 20
        ),
    )(dq, dk, dv, table, low, hidden, up_query, up_value)


def finish_kernel(gq, gk, gv, done, oq, ok, ov, qd, qu, vd, vu, sems):
    copies = [
        pltpu.make_async_copy(src, dst, sems.at[index])
        for index, (src, dst) in enumerate(((gq, oq), (gk, ok), (gv, ov)))
    ]
    for copy in copies:
        copy.start()
    d_tiles = qd.shape[1] // 128
    for column in range(d_tiles):
        cols = slice(column * 128, (column + 1) * 128)
        qd[:, cols] = done[2 * column]
        vd[:, cols] = done[2 * column + 1]
    for column in range(qu.shape[1] // 128):
        cols = slice(column * 128, (column + 1) * 128)
        qu[:, cols] = done[2 * (d_tiles + column)]
        vu[:, cols] = done[2 * (d_tiles + column) + 1]
    for copy in copies:
        copy.wait()


def write_results(gq, gk, gv, done, model):
    rows, width = gq.shape
    vmem = pl.BlockSpec(memory_space=pltpu.VMEM)
    hbm = pl.BlockSpec(memory_space=pltpu.HBM)
    grad = jax.ShapeDtypeStruct((rows, width), BF16)
    down = jax.ShapeDtypeStruct((RANK, model // 8), F32)
    up = jax.ShapeDtypeStruct((RANK, width // 8), F32)
    return pl.pallas_call(
        finish_kernel,
        name="write_results",
        out_shape=(grad, grad, grad, down, up, down, up),
        in_specs=[vmem] * 4,
        out_specs=[hbm] * 3 + [vmem] * 4,
        scratch_shapes=[pltpu.SemaphoreType.DMA((3,))],
        compiler_params=pltpu.CompilerParams(vmem_limit_bytes=4 << 20),
    )(gq, gk, gv, done)


def shards(
    hidden,
    queries,
    key_states,
    value_states,
    attention_out,
    grad_out,
    lengths,
    down_query,
    up_query,
    down_value,
    up_value,
):
    q, k, v, g, delta, low, lse, kt, table = gather_heads(
        lengths, queries, key_states, value_states, grad_out, attention_out, hidden, down_query, down_value
    )
    dq, dk, dv = attention_backward(lengths, q, k, v, g, delta, lse, kt)
    gq, gk, gv, done = return_heads(dq, dk, dv, table, low, hidden, up_query, up_value)
    return write_results(gq, gk, gv, done, hidden.shape[1])


def solution(mesh):
    tokens = P(("dp", "seq"), None)
    return jax.shard_map(
        shards,
        mesh=mesh,
        in_specs=(tokens,) * 6 + (P("dp", None), P(), P(), P(), P()),
        out_specs=(tokens,) * 3 + (P(None, "dp"),) * 4,
        check_vma=False,
    )
```

```python
import math

import jax
import jax.numpy as jnp
from jax import lax
from jax.experimental import pallas as pl
from jax.experimental.pallas import tpu as pltpu
from jax.sharding import PartitionSpec as P

H = 32
HD = 128
RANK = 8
ADAPTER_SCALE = 2.0
BQ = 512
BK = 512
GATHER_MIB = 48
LONGEST = 2048
SCALING = 1.0 / math.sqrt(HD)
TO_LOG2 = SCALING * math.log2(math.e)
MESH = pl.DeviceIdType.MESH
NT = (((1,), (1,)), ((), ()))
F32 = jnp.float32
BF16 = jnp.bfloat16


def nt_dot(a, b):
    return lax.dot_general(a, b, NT, preferred_element_type=F32)


def starts_of(len_ref):
    first = len_ref[0, 0]
    second = first + len_ref[0, 1]
    third = second + len_ref[0, 2]
    return first, second, third


def begin_of(positions, starts):
    found = jnp.zeros_like(positions)
    for start in starts:
        found = jnp.where(positions >= start, start, found)
    return found


def partners(me):
    xs = [lax.rem(lax.div(me, 8) + d, 4) * 8 for d in range(4)]
    ys = [lax.rem(lax.div(me, 2) + d, 4) * 2 for d in range(4)]
    cores = [lax.rem(me + d, 2) for d in range(2)]
    chips = [step % 16 * 7 % 16 for step in range(32)]
    return [xs[chips[step] // 4] + ys[chips[step] % 4] + cores[step // 16] for step in range(32)]


def bytes_of(ref, send_sem, recv_sem, other):
    return pltpu.make_async_remote_copy(
        src_ref=ref, dst_ref=ref, send_sem=send_sem, recv_sem=recv_sem,
        device_id={"seq": other}, device_id_type=MESH,
    )


def gather_kernel(
    len_ref, q_ref, k_ref, v_ref, g_ref, o_ref, hid_ref, downq, downv,
    hq, hk, hv, hg, hd, hlow, lse, kt, table_ref,
    g_buf, o_buf, hid, wq, wv, d_buf, low, table, stat, send, recv, local, load,
):
    members = 32
    me = lax.axis_index("seq")
    rows = q_ref.shape[0]
    others = partners(me)
    barrier = pltpu.get_barrier_semaphore()
    for step in range(1, members):
        pl.semaphore_signal(barrier, inc=1, device_id={"seq": others[step]}, device_id_type=MESH)
    loads = [
        pltpu.make_async_copy(src, dst, load.at[index])
        for index, (src, dst) in enumerate(
            ((g_ref, g_buf), (o_ref, o_buf), (hid_ref, hid), (downq, wq), (downv, wv))
        )
    ]
    for copy in loads:
        copy.start()
    pairs = ((q_ref, hq), (k_ref, hk), (v_ref, hv), (g_ref, hg))
    my_rows = pl.ds(pl.multiple_of(me * rows, rows), rows)

    def columns(member):
        return pl.ds(pl.multiple_of(member * HD, HD), HD)

    own = [
        pltpu.make_async_copy(src.at[:, columns(me)], dst.at[my_rows, :], local.at[index])
        for index, (src, dst) in enumerate(pairs)
    ]
    for copy in own:
        copy.start()
    pl.semaphore_wait(barrier, members - 1)

    def copies(other, indices):
        moves = [(src.at[:, columns(other)], dst.at[my_rows, :]) for src, dst in pairs]
        moves.append((d_buf.at[other], hd.at[me]))
        moves.append((low, hlow.at[:, columns(me)]))
        return [
            pltpu.make_async_remote_copy(
                src_ref=src,
                dst_ref=dst,
                send_sem=send.at[index],
                recv_sem=recv.at[index],
                device_id={"seq": other},
                device_id_type=MESH,
            )
            for index, (src, dst) in enumerate(moves)
            if index in indices
        ]

    def start(indices):
        for step in range(1, members):
            for copy in copies(others[step], indices):
                copy.start()

    start((0, 1))
    for copy in loads:
        copy.wait()

    def delta_of(head, _):
        cols = columns(head)
        product = g_buf[:, cols].astype(F32) * o_buf[:, cols].astype(F32)
        d_buf[head] = jnp.sum(product.T, axis=0, keepdims=True)
        return 0

    lax.fori_loop(0, H, delta_of, 0)
    low[0:8, :] = nt_dot(wq[...], hid[...]).astype(BF16)
    low[8:16, :] = nt_dot(wv[...], hid[...]).astype(BF16)
    own_small = [
        pltpu.make_async_copy(d_buf.at[me], hd.at[me], local.at[4]),
        pltpu.make_async_copy(low, hlow.at[:, columns(me)], local.at[5]),
    ]
    for copy in own_small:
        copy.start()

    start((4, 5))
    start((2, 3))

    starts = starts_of(len_ref)
    lane = lax.broadcasted_iota(jnp.int32, (rows, HD), 1)
    pair = jnp.where(lane >= HD // 2, lane - HD // 2, lane).astype(F32)
    inverse = jnp.exp(-(pair * (2.0 / HD)) * math.log(10000.0))

    def angles(block, _):
        at = pl.multiple_of(block * rows, rows)
        token = at + lax.broadcasted_iota(jnp.int32, (rows, HD), 0)
        angle = (token - begin_of(token, starts)).astype(F32) * inverse
        table[pl.ds(at, rows), :] = jnp.where(lane >= HD // 2, jnp.sin(angle), jnp.cos(angle))
        return 0

    lax.fori_loop(0, members, angles, 0)
    store = pltpu.make_async_copy(table, table_ref, load.at[5])
    store.start()
    for copy in own + own_small:
        copy.wait()

    slots = members - 1
    landed = [dst.at[pl.ds(0, slots * rows), :] for _, dst in pairs]
    landed += [hd.at[pl.ds(0, slots)], hlow.at[:, pl.ds(0, slots * rows)]]
    moved = [bytes_of(ref, send.at[index], recv.at[index], others[1]) for index, ref in enumerate(landed)]
    moved[0].wait_recv()
    moved[1].wait_recv()
    total = hq.shape[0]

    def turn(block, _):
        at = pl.multiple_of(block * 256, 256)
        kt[:, pl.ds(at, 256)] = hk[pl.ds(at, 256), :].T
        return 0

    lax.fori_loop(0, total // 256, turn, 0)

    def statistics(query_block, _):
        q0 = pl.multiple_of(query_block * BQ, BQ)
        q_rows = hq[pl.ds(q0, BQ), :]
        query_at = q0 + lax.broadcasted_iota(jnp.int32, (1, BQ), 1)
        query_begin = begin_of(query_at, starts)
        stat[0] = jnp.full((8, BQ), -1e30, F32)
        stat[1] = jnp.zeros((8, BQ), F32)

        def block(k0, diagonal):
            key_at = k0 + lax.broadcasted_iota(jnp.int32, (BQ, BQ), 0)
            allowed = key_at >= query_begin
            if diagonal:
                allowed = jnp.logical_and(allowed, key_at <= query_at)
            s = jnp.where(allowed, nt_dot(hk[pl.ds(k0, BQ), :], q_rows), -1e30)
            s = s.reshape(BQ // 8, 8, BQ)
            old = stat[0]
            new = jnp.maximum(old, jnp.max(s, axis=0))
            stat[0] = new
            stat[1] = stat[1] * jnp.exp2((old - new) * TO_LOG2) + jnp.sum(jnp.exp2((s - new[None]) * TO_LOG2), axis=0)

        def earlier(key_block, _):
            block(pl.multiple_of(key_block * BQ, BQ), False)
            return 0

        lax.fori_loop(jnp.maximum(query_block - LONGEST // BQ, 0), query_block, earlier, 0)
        block(q0, True)
        top = jnp.max(stat[0], axis=0, keepdims=True)
        weight = jnp.sum(stat[1] * jnp.exp2((stat[0] - top) * TO_LOG2), axis=0, keepdims=True)
        lse[query_block] = top * TO_LOG2 + jnp.log2(weight)
        return 0

    lax.fori_loop(0, total // BQ, statistics, 0)

    moved[0].wait_send()
    moved[1].wait_send()
    for copy in moved[2:]:
        copy.wait()
    store.wait()


def gather_heads(lengths, queries, key_states, value_states, grad_out, attention_out, hidden, down_query, down_value):
    rows, width = queries.shape
    model = hidden.shape[1]
    hbm = pl.BlockSpec(memory_space=pltpu.HBM)
    vmem = pl.BlockSpec(memory_space=pltpu.VMEM)
    total = rows * 32
    head = jax.ShapeDtypeStruct((total, HD), BF16)
    return pl.pallas_call(
        gather_kernel,
        name="gather_heads",
        out_shape=(
            head, head, head, head,
            jax.ShapeDtypeStruct((32, 1, rows), F32),
            jax.ShapeDtypeStruct((2 * RANK, total), BF16),
            jax.ShapeDtypeStruct((total // BQ, 1, BQ), F32),
            jax.ShapeDtypeStruct((HD, total), BF16),
            jax.ShapeDtypeStruct((total, HD), F32),
        ),
        in_specs=[pl.BlockSpec(memory_space=pltpu.SMEM)] + [hbm] * 8,
        out_specs=[vmem] * 8 + [hbm],
        scratch_shapes=[
            pltpu.VMEM((rows, width), BF16),
            pltpu.VMEM((rows, width), BF16),
            pltpu.VMEM((rows, model), BF16),
            pltpu.VMEM((RANK, model), BF16),
            pltpu.VMEM((RANK, model), BF16),
            pltpu.VMEM((H, 1, rows), F32),
            pltpu.VMEM((2 * RANK, rows), BF16),
            pltpu.VMEM((total, HD), F32),
            pltpu.VMEM((2, 8, BQ), F32),
            pltpu.SemaphoreType.DMA((6,)),
            pltpu.SemaphoreType.DMA((6,)),
            pltpu.SemaphoreType.DMA((6,)),
            pltpu.SemaphoreType.DMA((6,)),
        ],
        compiler_params=pltpu.CompilerParams(
            collective_id=0, has_side_effects=True, vmem_limit_bytes=GATHER_MIB << 20
        ),
    )(lengths, queries, key_states, value_states, grad_out, attention_out, hidden, down_query, down_value)


def attention_kernel(
    len_ref, q_ref, k_ref, v_ref, g_ref, d_ref, lse_ref, kt, dq_ref, dk_ref, dv_ref, dk_acc, dv_acc, dq_acc
):
    total = q_ref.shape[0]
    starts = starts_of(len_ref)
    dk_acc[...] = jnp.zeros_like(dk_acc)
    dv_acc[...] = jnp.zeros_like(dv_acc)

    def outer(query_block, _):
        q0 = pl.multiple_of(query_block * BQ, BQ)
        q_rows = q_ref[pl.ds(q0, BQ), :]
        g_rows = g_ref[pl.ds(q0, BQ), :]
        delta = jnp.concatenate([d_ref[query_block * (BQ // 128) + i] for i in range(BQ // 128)], axis=1)
        lse = lse_ref[query_block]
        query_at = q0 + lax.broadcasted_iota(jnp.int32, (1, BQ), 1)
        query_begin = begin_of(query_at, starts)
        low = begin_of(q0, starts)
        high = begin_of(q0 + (BQ - 1), starts)
        first = lax.div(low, BK)
        last = lax.div(q0 + (BQ - 1), BK) + 1
        dq_acc[...] = jnp.zeros_like(dq_acc)

        def pair(key_block, _):
            k0 = pl.multiple_of(key_block * BK, BK)
            rows = pl.ds(k0, BK)
            inside = jnp.logical_and(high <= k0, k0 + (BK - 1) <= q0)

            def spread(s):
                weight = jnp.exp2(s * TO_LOG2 - lse)
                p = weight.astype(BF16)
                ds = (weight * (nt_dot(v_ref[rows, :], g_rows) - delta)).astype(BF16)
                dv_acc[rows, :] += jnp.dot(p, g_rows, preferred_element_type=F32)
                dk_acc[rows, :] += jnp.dot(ds, q_rows, preferred_element_type=F32)
                dq_acc[...] += jnp.dot(kt[:, rows], ds, preferred_element_type=F32)

            @pl.when(inside)
            def _():
                spread(nt_dot(k_ref[rows, :], q_rows))

            @pl.when(jnp.logical_not(inside))
            def _():
                key_at = k0 + lax.broadcasted_iota(jnp.int32, (BK, BQ), 0)
                allowed = jnp.logical_and(key_at >= query_begin, key_at <= query_at)
                spread(jnp.where(allowed, nt_dot(k_ref[rows, :], q_rows), -1e30))

            return 0

        lax.fori_loop(first, last, pair, 0)
        dq_ref[pl.ds(q0, BQ), :] = (dq_acc[...] * SCALING).T.astype(BF16)
        return 0

    lax.fori_loop(0, total // BQ, outer, 0)
    dk_ref[...] = (dk_acc[...] * SCALING).astype(BF16)
    dv_ref[...] = dv_acc[...].astype(BF16)


def attention_backward(lengths, q, k, v, g, delta, lse, kt):
    total = q.shape[0]
    vmem = pl.BlockSpec(memory_space=pltpu.VMEM)
    head = jax.ShapeDtypeStruct((total, HD), BF16)
    return pl.pallas_call(
        attention_kernel,
        name="attention_backward",
        out_shape=(head, head, head),
        in_specs=[pl.BlockSpec(memory_space=pltpu.SMEM)] + [vmem] * 7,
        out_specs=[vmem] * 3,
        scratch_shapes=[
            pltpu.VMEM((total, HD), F32),
            pltpu.VMEM((total, HD), F32),
            pltpu.VMEM((HD, BQ), F32),
        ],
        compiler_params=pltpu.CompilerParams(vmem_limit_bytes=20 << 20),
    )(lengths, q, k, v, g, delta, lse, kt)


def return_kernel(
    dq_ref, dk_ref, dv_ref, table, low, hid, upq, upv,
    gq_ref, gk_ref, gv_ref, done,
    back_out, back_in, part, z_in, up_part, up_in, tiles, r_in,
    send, recv, local, b_send, b_recv, z_send, z_recv, u_send, u_recv, r_send, r_recv, a_send, a_recv, c_send, c_recv,
):
    members, groups = 32, 8
    me = lax.axis_index("seq")
    dp = lax.axis_index("dp")
    rows = gq_ref.shape[0]
    total = dq_ref.shape[0]
    d_cols = hid.shape[1] // groups
    n_tiles = 2 * d_cols // 128
    chunk = 512
    barrier = pltpu.get_barrier_semaphore()

    def across(step):
        return lax.rem(dp + step, groups)

    others = partners(me)
    for step in range(1, members):
        pl.semaphore_signal(barrier, inc=1, device_id={"seq": others[step]}, device_id_type=MESH)
    for step in range(1, groups):
        pl.semaphore_signal(barrier, inc=1, device_id={"dp": across(step)}, device_id_type=MESH)
    pairs = ((dq_ref, gq_ref), (dv_ref, gv_ref), (dk_ref, gk_ref))
    my_cols = pl.ds(pl.multiple_of(me * HD, HD), HD)

    def rows_of(member):
        return pl.ds(pl.multiple_of(member * rows, rows), rows)

    own = [
        pltpu.make_async_copy(src.at[rows_of(me), :], dst.at[:, my_cols], local.at[index])
        for index, (src, dst) in enumerate(pairs)
    ]
    for copy in own:
        copy.start()
    pl.semaphore_wait(barrier, members - 1 + groups - 1)

    def to_member(src, dst, send_sem, recv_sem, other):
        return pltpu.make_async_remote_copy(
            src_ref=src, dst_ref=dst, send_sem=send_sem, recv_sem=recv_sem,
            device_id={"seq": other}, device_id_type=MESH,
        )

    def to_group(src, dst, send_sem, recv_sem, other):
        return pltpu.make_async_remote_copy(
            src_ref=src, dst_ref=dst, send_sem=send_sem, recv_sem=recv_sem,
            device_id={"dp": other}, device_id_type=MESH,
        )

    def bulk(index, other):
        src, dst = pairs[index]
        return to_member(
            src.at[rows_of(other), :], dst.at[:, my_cols], send.at[index], recv.at[index], other
        )

    near = range(1, members // 2)
    far = range(members // 2, members)

    def start_bulk(index, steps):
        for step in steps:
            bulk(index, others[step]).start()

    start_bulk(0, near)

    up_q = upq[:, my_cols]
    up_v = upv[:, my_cols]

    def share(block, sums):
        sum_q, sum_v = sums
        at = pl.multiple_of(block * chunk, chunk)
        here = pl.ds(at, chunk)
        wave = table[here, :]
        other_half = pltpu.roll(wave, HD // 2, 1)
        first = lax.broadcasted_iota(jnp.int32, (chunk, HD), 1) < HD // 2
        cosine = jnp.where(first, wave, other_half)
        sine = jnp.where(first, other_half, -wave)
        x = dq_ref[here, :].astype(F32)
        pre = (x * cosine + pltpu.roll(x, HD // 2, 1) * sine).astype(BF16)
        value = dv_ref[here, :]
        back_q = nt_dot(up_q, pre)
        back_v = nt_dot(up_v, value)
        for piece in range(chunk // rows):
            cols = slice(piece * rows, (piece + 1) * rows)
            back_out[block * (chunk // rows) + piece, 0:8, :] = back_q[:, cols]
            back_out[block * (chunk // rows) + piece, 8:16, :] = back_v[:, cols]
        low_q = low[0:8, here]
        low_v = low[8:16, here]
        return (
            sum_q + jnp.dot(low_q, pre, preferred_element_type=F32),
            sum_v + jnp.dot(low_v, value, preferred_element_type=F32),
        )

    zero = jnp.zeros((8, HD), F32)
    sum_q, sum_v = lax.fori_loop(0, total // chunk, share, (zero, zero))
    up_part[0] = sum_q
    up_part[1] = sum_v

    def back(step, other):
        return to_member(back_out.at[other], back_in.at[step - 1], b_send, b_recv, other)

    for step in range(1, members):
        back(step, others[step]).start()
    owner = lax.div(me, members // groups)
    up_move = to_group(up_part, up_in.at[dp], u_send.at[dp], u_recv.at[dp], owner)

    @pl.when(owner != dp)
    def _():
        up_move.start()

    start_bulk(0, far)

    slots = members - 1
    backs = bytes_of(back_in.at[pl.ds(0, slots)], b_send, b_recv, others[1])
    backs.wait_recv()
    back_low = jnp.sum(back_in[0:slots], axis=0) + back_out[me]
    back_low = back_low.astype(BF16)

    def fill(group):
        cols = pl.ds(pl.multiple_of(group * d_cols, 128), d_cols)
        part[group] = jnp.dot(back_low, hid[:, cols], preferred_element_type=F32)

    def exchange(step):
        other = across(step)
        return to_group(part.at[other], z_in.at[step], z_send.at[step], z_recv.at[step], other)

    for step in range(1, groups):
        fill(across(step))
        exchange(step).start()
    start_bulk(1, near)
    start_bulk(1, far)
    fill(dp)

    def place_of(member):
        return pl.ds(n_tiles + 2 * lax.rem(member, members // groups), 2)

    def spread_up(step, other):
        mine = done.at[place_of(me)]
        return to_member(mine, mine, c_send, c_recv, other)

    @pl.when(owner == dp)
    def _():
        summed = up_part[...]
        for step in range(1, groups):
            source = across(step)
            to_group(up_part, up_in.at[source], u_send.at[source], u_recv.at[source], source).wait_recv()
            summed = summed + up_in[source]
        done[place_of(me)] = summed * ADAPTER_SCALE

        for step in range(1, members):
            spread_up(step, others[step]).start()

    down = part[dp]
    for step in range(1, groups):
        exchange(step).wait()
        down = down + z_in[step]
    for tile in range(n_tiles):
        column, half = tile // 2, tile % 2
        tiles[tile] = down[half * 8:half * 8 + 8, column * 128:(column + 1) * 128]

    def scatter(step, other):
        return to_member(
            tiles.at[lax.rem(other, n_tiles)], r_in.at[step - 1], r_send, r_recv, other
        )

    def spread(step, other):
        mine = done.at[lax.rem(me, n_tiles)]
        return to_member(mine, mine, a_send, a_recv, other)

    for step in range(1, members):
        @pl.when(others[step] < n_tiles)
        def _(step=step):
            scatter(step, others[step]).start()

    start_bulk(2, near)

    @pl.when(me < n_tiles)
    def _():
        bytes_of(r_in, r_send, r_recv, others[1]).wait_recv()
        done[me] = (tiles[me] + jnp.sum(r_in[...], axis=0)) * ADAPTER_SCALE
        for step in range(1, members):
            spread(step, others[step]).start()

    start_bulk(2, far)

    backs.wait_send()

    @pl.when(me < n_tiles)
    def _():
        bytes_of(tiles.at[pl.ds(0, n_tiles - 1)], r_send, r_recv, others[1]).wait_send()
        bytes_of(r_in, a_send, a_recv, others[1]).wait_send()
        bytes_of(tiles.at[pl.ds(0, n_tiles - 1)], a_send, a_recv, others[1]).wait_recv()

    @pl.when(me >= n_tiles)
    def _():
        bytes_of(tiles, r_send, r_recv, others[1]).wait_send()
        bytes_of(tiles, a_send, a_recv, others[1]).wait_recv()

    per_group = members // groups

    @pl.when(owner == dp)
    def _():
        bytes_of(back_in.at[pl.ds(0, slots)], c_send, c_recv, others[1]).wait_send()
        bytes_of(up_in.at[pl.ds(0, per_group - 1)], c_send, c_recv, others[1]).wait_recv()

    @pl.when(owner != dp)
    def _():
        bytes_of(up_in.at[pl.ds(0, per_group)], c_send, c_recv, others[1]).wait_recv()

    for index, (_, dst) in enumerate(pairs):
        bytes_of(dst.at[:, pl.ds(0, slots * HD)], send.at[index], recv.at[index], others[1]).wait()

    @pl.when(owner != dp)
    def _():
        up_move.wait_send()

    for copy in own:
        copy.wait()


def return_heads(dq, dk, dv, table, low, hidden, up_query, up_value):
    rows, model = hidden.shape
    total = dq.shape[0]
    width = up_query.shape[1]
    vmem = pl.BlockSpec(memory_space=pltpu.VMEM)
    grad = jax.ShapeDtypeStruct((rows, width), BF16)
    d_cols = model // 8
    n_tiles = 2 * d_cols // 128
    all_tiles = n_tiles + 2 * (width // 8) // 128
    dma = pltpu.SemaphoreType.DMA
    return pl.pallas_call(
        return_kernel,
        name="return_heads",
        out_shape=(grad, grad, grad, jax.ShapeDtypeStruct((all_tiles, 8, 128), F32)),
        in_specs=[vmem] * 8,
        out_specs=[vmem] * 4,
        scratch_shapes=[
            pltpu.VMEM((32, 2 * RANK, rows), F32),
            pltpu.VMEM((32, 2 * RANK, rows), F32),
            pltpu.VMEM((8, 2 * RANK, d_cols), F32),
            pltpu.VMEM((8, 2 * RANK, d_cols), F32),
            pltpu.VMEM((2, RANK, HD), F32),
            pltpu.VMEM((8, 2, RANK, HD), F32),
            pltpu.VMEM((n_tiles, 8, 128), F32),
            pltpu.VMEM((31, 8, 128), F32),
            dma((3,)), dma((3,)), dma((3,)),
            dma, dma,
            dma((8,)), dma((8,)),
            dma((8,)), dma((8,)),
            dma, dma,
            dma, dma,
            dma, dma,
        ],
        compiler_params=pltpu.CompilerParams(
            collective_id=1, has_side_effects=True, vmem_limit_bytes=16 << 20
        ),
    )(dq, dk, dv, table, low, hidden, up_query, up_value)


def finish_kernel(gq, gk, gv, done, oq, ok, ov, qd, qu, vd, vu, sems):
    copies = [
        pltpu.make_async_copy(src, dst, sems.at[index])
        for index, (src, dst) in enumerate(((gq, oq), (gk, ok), (gv, ov)))
    ]
    for copy in copies:
        copy.start()
    d_tiles = qd.shape[1] // 128
    for column in range(d_tiles):
        cols = slice(column * 128, (column + 1) * 128)
        qd[:, cols] = done[2 * column]
        vd[:, cols] = done[2 * column + 1]
    for column in range(qu.shape[1] // 128):
        cols = slice(column * 128, (column + 1) * 128)
        qu[:, cols] = done[2 * (d_tiles + column)]
        vu[:, cols] = done[2 * (d_tiles + column) + 1]
    for copy in copies:
        copy.wait()


def write_results(gq, gk, gv, done, model):
    rows, width = gq.shape
    vmem = pl.BlockSpec(memory_space=pltpu.VMEM)
    hbm = pl.BlockSpec(memory_space=pltpu.HBM)
    grad = jax.ShapeDtypeStruct((rows, width), BF16)
    down = jax.ShapeDtypeStruct((RANK, model // 8), F32)
    up = jax.ShapeDtypeStruct((RANK, width // 8), F32)
    return pl.pallas_call(
        finish_kernel,
        name="write_results",
        out_shape=(grad, grad, grad, down, up, down, up),
        in_specs=[vmem] * 4,
        out_specs=[hbm] * 3 + [vmem] * 4,
        scratch_shapes=[pltpu.SemaphoreType.DMA((3,))],
        compiler_params=pltpu.CompilerParams(vmem_limit_bytes=4 << 20),
    )(gq, gk, gv, done)


def shards(
    hidden,
    queries,
    key_states,
    value_states,
    attention_out,
    grad_out,
    lengths,
    down_query,
    up_query,
    down_value,
    up_value,
):
    q, k, v, g, delta, low, lse, kt, table = gather_heads(
        lengths, queries, key_states, value_states, grad_out, attention_out, hidden, down_query, down_value
    )
    dq, dk, dv = attention_backward(lengths, q, k, v, g, delta, lse, kt)
    gq, gk, gv, done = return_heads(dq, dk, dv, table, low, hidden, up_query, up_value)
    return write_results(gq, gk, gv, done, hidden.shape[1])


def solution(mesh):
    tokens = P(("dp", "seq"), None)
    return jax.shard_map(
        shards,
        mesh=mesh,
        in_specs=(tokens,) * 6 + (P("dp", None), P(), P(), P(), P()),
        out_specs=(tokens,) * 3 + (P(None, "dp"),) * 4,
        check_vma=False,
    )
```

```python
import math

import jax
import jax.numpy as jnp
from jax import lax
from jax.experimental import pallas as pl
from jax.experimental.pallas import tpu as pltpu
from jax.sharding import PartitionSpec as P

H = 32
HD = 128
RANK = 8
ADAPTER_SCALE = 2.0
BQ = 512
BK = 512
GATHER_MIB = 48
LONGEST = 2048
SCALING = 1.0 / math.sqrt(HD)
TO_LOG2 = SCALING * math.log2(math.e)
MESH = pl.DeviceIdType.MESH
NT = (((1,), (1,)), ((), ()))
F32 = jnp.float32
BF16 = jnp.bfloat16


def nt_dot(a, b):
    return lax.dot_general(a, b, NT, preferred_element_type=F32)


def starts_of(len_ref):
    first = len_ref[0, 0]
    second = first + len_ref[0, 1]
    third = second + len_ref[0, 2]
    return first, second, third


def begin_of(positions, starts):
    found = jnp.zeros_like(positions)
    for start in starts:
        found = jnp.where(positions >= start, start, found)
    return found


def partners(me):
    xs = [lax.rem(lax.div(me, 8) + d, 4) * 8 for d in range(4)]
    ys = [lax.rem(lax.div(me, 2) + d, 4) * 2 for d in range(4)]
    cores = [lax.rem(me + d, 2) for d in range(2)]
    chips = [step % 16 * 7 % 16 for step in range(32)]
    return [xs[chips[step] // 4] + ys[chips[step] % 4] + cores[step // 16] for step in range(32)]


def bytes_of(ref, send_sem, recv_sem, other):
    return pltpu.make_async_remote_copy(
        src_ref=ref, dst_ref=ref, send_sem=send_sem, recv_sem=recv_sem,
        device_id={"seq": other}, device_id_type=MESH,
    )


def gather_kernel(
    len_ref, q_ref, k_ref, v_ref, g_ref, o_ref, hid_ref, downq, downv,
    hq, hk, hv, hg, hd, hlow, lse, kt, table_ref,
    g_buf, o_buf, hid, wq, wv, d_buf, low, table, stat, send, recv, local, load,
):
    members = 32
    me = lax.axis_index("seq")
    rows = q_ref.shape[0]
    others = partners(me)
    barrier = pltpu.get_barrier_semaphore()
    for step in range(1, members):
        pl.semaphore_signal(barrier, inc=1, device_id={"seq": others[step]}, device_id_type=MESH)
    loads = [
        pltpu.make_async_copy(src, dst, load.at[index])
        for index, (src, dst) in enumerate(
            ((g_ref, g_buf), (o_ref, o_buf), (hid_ref, hid), (downq, wq), (downv, wv))
        )
    ]
    for copy in loads:
        copy.start()
    pairs = ((q_ref, hq), (k_ref, hk), (v_ref, hv), (g_ref, hg))
    my_rows = pl.ds(pl.multiple_of(me * rows, rows), rows)

    def columns(member):
        return pl.ds(pl.multiple_of(member * HD, HD), HD)

    own = [
        pltpu.make_async_copy(src.at[:, columns(me)], dst.at[my_rows, :], local.at[index])
        for index, (src, dst) in enumerate(pairs)
    ]
    for copy in own:
        copy.start()
    pl.semaphore_wait(barrier, members - 1)

    def copies(other, indices):
        moves = [(src.at[:, columns(other)], dst.at[my_rows, :]) for src, dst in pairs]
        moves.append((d_buf.at[other], hd.at[me]))
        moves.append((low, hlow.at[:, columns(me)]))
        return [
            pltpu.make_async_remote_copy(
                src_ref=src,
                dst_ref=dst,
                send_sem=send.at[index],
                recv_sem=recv.at[index],
                device_id={"seq": other},
                device_id_type=MESH,
            )
            for index, (src, dst) in enumerate(moves)
            if index in indices
        ]

    def start(indices):
        for step in range(1, members):
            for copy in copies(others[step], indices):
                copy.start()

    start((0, 1))
    for copy in loads:
        copy.wait()

    def delta_of(head, _):
        cols = columns(head)
        product = g_buf[:, cols].astype(F32) * o_buf[:, cols].astype(F32)
        d_buf[head] = jnp.sum(product.T, axis=0, keepdims=True)
        return 0

    lax.fori_loop(0, H, delta_of, 0)
    low[0:8, :] = nt_dot(wq[...], hid[...]).astype(BF16)
    low[8:16, :] = nt_dot(wv[...], hid[...]).astype(BF16)
    own_small = [
        pltpu.make_async_copy(d_buf.at[me], hd.at[me], local.at[4]),
        pltpu.make_async_copy(low, hlow.at[:, columns(me)], local.at[5]),
    ]
    for copy in own_small:
        copy.start()

    start((4, 5))
    start((2, 3))

    starts = starts_of(len_ref)
    lane = lax.broadcasted_iota(jnp.int32, (rows, HD), 1)
    pair = jnp.where(lane >= HD // 2, lane - HD // 2, lane).astype(F32)
    inverse = jnp.exp(-(pair * (2.0 / HD)) * math.log(10000.0))

    def angles(block, _):
        at = pl.multiple_of(block * rows, rows)
        token = at + lax.broadcasted_iota(jnp.int32, (rows, HD), 0)
        angle = (token - begin_of(token, starts)).astype(F32) * inverse
        table[pl.ds(at, rows), :] = jnp.where(lane >= HD // 2, jnp.sin(angle), jnp.cos(angle))
        return 0

    lax.fori_loop(0, members, angles, 0)
    store = pltpu.make_async_copy(table, table_ref, load.at[5])
    store.start()
    for copy in own + own_small:
        copy.wait()

    slots = members - 1
    landed = [dst.at[pl.ds(0, slots * rows), :] for _, dst in pairs]
    landed += [hd.at[pl.ds(0, slots)], hlow.at[:, pl.ds(0, slots * rows)]]
    moved = [bytes_of(ref, send.at[index], recv.at[index], others[1]) for index, ref in enumerate(landed)]
    moved[0].wait_recv()
    moved[1].wait_recv()
    total = hq.shape[0]

    def turn(block, _):
        at = pl.multiple_of(block * 256, 256)
        kt[:, pl.ds(at, 256)] = hk[pl.ds(at, 256), :].T
        return 0

    lax.fori_loop(0, total // 256, turn, 0)

    def statistics(query_block, _):
        q0 = pl.multiple_of(query_block * BQ, BQ)
        q_rows = hq[pl.ds(q0, BQ), :]
        query_at = q0 + lax.broadcasted_iota(jnp.int32, (1, BQ), 1)
        query_begin = begin_of(query_at, starts)
        stat[0] = jnp.full((8, BQ), -1e30, F32)
        stat[1] = jnp.zeros((8, BQ), F32)

        def block(k0, diagonal):
            key_at = k0 + lax.broadcasted_iota(jnp.int32, (BQ, BQ), 0)
            allowed = key_at >= query_begin
            if diagonal:
                allowed = jnp.logical_and(allowed, key_at <= query_at)
            s = jnp.where(allowed, nt_dot(hk[pl.ds(k0, BQ), :], q_rows), -1e30)
            s = s.reshape(BQ // 8, 8, BQ)
            old = stat[0]
            new = jnp.maximum(old, jnp.max(s, axis=0))
            stat[0] = new
            stat[1] = stat[1] * jnp.exp2((old - new) * TO_LOG2) + jnp.sum(jnp.exp2((s - new[None]) * TO_LOG2), axis=0)

        def earlier(key_block, _):
            block(pl.multiple_of(key_block * BQ, BQ), False)
            return 0

        lax.fori_loop(jnp.maximum(query_block - LONGEST // BQ, 0), query_block, earlier, 0)
        block(q0, True)
        top = jnp.max(stat[0], axis=0, keepdims=True)
        weight = jnp.sum(stat[1] * jnp.exp2((stat[0] - top) * TO_LOG2), axis=0, keepdims=True)
        lse[query_block] = top * TO_LOG2 + jnp.log2(weight)
        return 0

    lax.fori_loop(0, total // BQ, statistics, 0)

    moved[0].wait_send()
    moved[1].wait_send()
    for copy in moved[2:]:
        copy.wait()
    store.wait()


def gather_heads(lengths, queries, key_states, value_states, grad_out, attention_out, hidden, down_query, down_value):
    rows, width = queries.shape
    model = hidden.shape[1]
    hbm = pl.BlockSpec(memory_space=pltpu.HBM)
    vmem = pl.BlockSpec(memory_space=pltpu.VMEM)
    total = rows * 32
    head = jax.ShapeDtypeStruct((total, HD), BF16)
    return pl.pallas_call(
        gather_kernel,
        name="gather_heads",
        out_shape=(
            head, head, head, head,
            jax.ShapeDtypeStruct((32, 1, rows), F32),
            jax.ShapeDtypeStruct((2 * RANK, total), BF16),
            jax.ShapeDtypeStruct((total // BQ, 1, BQ), F32),
            jax.ShapeDtypeStruct((HD, total), BF16),
            jax.ShapeDtypeStruct((total, HD), F32),
        ),
        in_specs=[pl.BlockSpec(memory_space=pltpu.SMEM)] + [hbm] * 8,
        out_specs=[vmem] * 8 + [hbm],
        scratch_shapes=[
            pltpu.VMEM((rows, width), BF16),
            pltpu.VMEM((rows, width), BF16),
            pltpu.VMEM((rows, model), BF16),
            pltpu.VMEM((RANK, model), BF16),
            pltpu.VMEM((RANK, model), BF16),
            pltpu.VMEM((H, 1, rows), F32),
            pltpu.VMEM((2 * RANK, rows), BF16),
            pltpu.VMEM((total, HD), F32),
            pltpu.VMEM((2, 8, BQ), F32),
            pltpu.SemaphoreType.DMA((6,)),
            pltpu.SemaphoreType.DMA((6,)),
            pltpu.SemaphoreType.DMA((6,)),
            pltpu.SemaphoreType.DMA((6,)),
        ],
        compiler_params=pltpu.CompilerParams(
            collective_id=0, has_side_effects=True, vmem_limit_bytes=GATHER_MIB << 20
        ),
    )(lengths, queries, key_states, value_states, grad_out, attention_out, hidden, down_query, down_value)


def attention_kernel(
    len_ref, q_ref, k_ref, v_ref, g_ref, d_ref, lse_ref, kt, dq_ref, dk_ref, dv_ref, dk_acc, dv_acc, dq_acc
):
    total = q_ref.shape[0]
    starts = starts_of(len_ref)
    dk_acc[...] = jnp.zeros_like(dk_acc)
    dv_acc[...] = jnp.zeros_like(dv_acc)

    def outer(query_block, _):
        q0 = pl.multiple_of(query_block * BQ, BQ)
        q_rows = q_ref[pl.ds(q0, BQ), :]
        g_rows = g_ref[pl.ds(q0, BQ), :]
        delta = jnp.concatenate([d_ref[query_block * (BQ // 128) + i] for i in range(BQ // 128)], axis=1)
        lse = lse_ref[query_block]
        query_at = q0 + lax.broadcasted_iota(jnp.int32, (1, BQ), 1)
        query_begin = begin_of(query_at, starts)
        low = begin_of(q0, starts)
        high = begin_of(q0 + (BQ - 1), starts)
        first = lax.div(low, BK)
        last = lax.div(q0 + (BQ - 1), BK) + 1
        dq_acc[...] = jnp.zeros_like(dq_acc)

        def pair(key_block, _):
            k0 = pl.multiple_of(key_block * BK, BK)
            rows = pl.ds(k0, BK)
            inside = jnp.logical_and(high <= k0, k0 + (BK - 1) <= q0)

            def spread(rows, skip, s):
                weight = jnp.exp2(s * TO_LOG2 - lse[:, skip:])
                p = weight.astype(BF16)
                grad_p = nt_dot(v_ref[rows, :], g_rows[skip:, :])
                ds = (weight * (grad_p - delta[:, skip:])).astype(BF16)
                dv_acc[rows, :] += jnp.dot(p, g_rows[skip:, :], preferred_element_type=F32)
                dk_acc[rows, :] += jnp.dot(ds, q_rows[skip:, :], preferred_element_type=F32)
                dq_acc[:, skip:] += jnp.dot(kt[:, rows], ds, preferred_element_type=F32)

            def masked(rows, key0, count, skip):
                key_at = key0 + lax.broadcasted_iota(jnp.int32, (count, BQ - skip), 0)
                allowed = jnp.logical_and(key_at >= query_begin[:, skip:], key_at <= query_at[:, skip:])
                return jnp.where(allowed, nt_dot(k_ref[rows, :], q_rows[skip:, :]), -1e30)

            diagonal = key_block == query_block

            @pl.when(inside)
            def _():
                spread(rows, 0, nt_dot(k_ref[rows, :], q_rows))

            @pl.when(jnp.logical_not(jnp.logical_or(inside, diagonal)))
            def _():
                spread(rows, 0, masked(rows, k0, BK, 0))

            @pl.when(diagonal)
            def _():
                for skip in (0, BQ // 2):
                    at = pl.multiple_of(k0 + skip, BQ // 2)
                    part = pl.ds(at, BQ // 2)
                    spread(part, skip, masked(part, at, BQ // 2, skip))

            return 0

        lax.fori_loop(first, last, pair, 0)
        dq_ref[pl.ds(q0, BQ), :] = (dq_acc[...] * SCALING).T.astype(BF16)
        return 0

    lax.fori_loop(0, total // BQ, outer, 0)
    dk_ref[...] = (dk_acc[...] * SCALING).astype(BF16)
    dv_ref[...] = dv_acc[...].astype(BF16)


def attention_backward(lengths, q, k, v, g, delta, lse, kt):
    total = q.shape[0]
    vmem = pl.BlockSpec(memory_space=pltpu.VMEM)
    head = jax.ShapeDtypeStruct((total, HD), BF16)
    return pl.pallas_call(
        attention_kernel,
        name="attention_backward",
        out_shape=(head, head, head),
        in_specs=[pl.BlockSpec(memory_space=pltpu.SMEM)] + [vmem] * 7,
        out_specs=[vmem] * 3,
        scratch_shapes=[
            pltpu.VMEM((total, HD), F32),
            pltpu.VMEM((total, HD), F32),
            pltpu.VMEM((HD, BQ), F32),
        ],
        compiler_params=pltpu.CompilerParams(vmem_limit_bytes=20 << 20),
    )(lengths, q, k, v, g, delta, lse, kt)


def return_kernel(
    dq_ref, dk_ref, dv_ref, table, low, hid, upq, upv,
    gq_ref, gk_ref, gv_ref, done,
    back_out, back_in, part, z_in, up_part, up_in, tiles, r_in,
    send, recv, local, b_send, b_recv, z_send, z_recv, u_send, u_recv, r_send, r_recv, a_send, a_recv, c_send, c_recv,
):
    members, groups = 32, 8
    me = lax.axis_index("seq")
    dp = lax.axis_index("dp")
    rows = gq_ref.shape[0]
    total = dq_ref.shape[0]
    d_cols = hid.shape[1] // groups
    n_tiles = 2 * d_cols // 128
    chunk = 512
    barrier = pltpu.get_barrier_semaphore()

    def across(step):
        return lax.rem(dp + step, groups)

    others = partners(me)
    for step in range(1, members):
        pl.semaphore_signal(barrier, inc=1, device_id={"seq": others[step]}, device_id_type=MESH)
    for step in range(1, groups):
        pl.semaphore_signal(barrier, inc=1, device_id={"dp": across(step)}, device_id_type=MESH)
    pairs = ((dq_ref, gq_ref), (dv_ref, gv_ref), (dk_ref, gk_ref))
    my_cols = pl.ds(pl.multiple_of(me * HD, HD), HD)

    def rows_of(member):
        return pl.ds(pl.multiple_of(member * rows, rows), rows)

    own = [
        pltpu.make_async_copy(src.at[rows_of(me), :], dst.at[:, my_cols], local.at[index])
        for index, (src, dst) in enumerate(pairs)
    ]
    for copy in own:
        copy.start()
    pl.semaphore_wait(barrier, members - 1 + groups - 1)

    def to_member(src, dst, send_sem, recv_sem, other):
        return pltpu.make_async_remote_copy(
            src_ref=src, dst_ref=dst, send_sem=send_sem, recv_sem=recv_sem,
            device_id={"seq": other}, device_id_type=MESH,
        )

    def to_group(src, dst, send_sem, recv_sem, other):
        return pltpu.make_async_remote_copy(
            src_ref=src, dst_ref=dst, send_sem=send_sem, recv_sem=recv_sem,
            device_id={"dp": other}, device_id_type=MESH,
        )

    def bulk(index, other):
        src, dst = pairs[index]
        return to_member(
            src.at[rows_of(other), :], dst.at[:, my_cols], send.at[index], recv.at[index], other
        )

    near = range(1, members // 2)
    far = range(members // 2, members)

    def start_bulk(index, steps):
        for step in steps:
            bulk(index, others[step]).start()

    start_bulk(0, near)

    up_q = upq[:, my_cols]
    up_v = upv[:, my_cols]

    def share(block, sums):
        sum_q, sum_v = sums
        at = pl.multiple_of(block * chunk, chunk)
        here = pl.ds(at, chunk)
        wave = table[here, :]
        other_half = pltpu.roll(wave, HD // 2, 1)
        first = lax.broadcasted_iota(jnp.int32, (chunk, HD), 1) < HD // 2
        cosine = jnp.where(first, wave, other_half)
        sine = jnp.where(first, other_half, -wave)
        x = dq_ref[here, :].astype(F32)
        pre = (x * cosine + pltpu.roll(x, HD // 2, 1) * sine).astype(BF16)
        value = dv_ref[here, :]
        back_q = nt_dot(up_q, pre)
        back_v = nt_dot(up_v, value)
        for piece in range(chunk // rows):
            cols = slice(piece * rows, (piece + 1) * rows)
            back_out[block * (chunk // rows) + piece, 0:8, :] = back_q[:, cols]
            back_out[block * (chunk // rows) + piece, 8:16, :] = back_v[:, cols]
        low_q = low[0:8, here]
        low_v = low[8:16, here]
        return (
            sum_q + jnp.dot(low_q, pre, preferred_element_type=F32),
            sum_v + jnp.dot(low_v, value, preferred_element_type=F32),
        )

    zero = jnp.zeros((8, HD), F32)
    sum_q, sum_v = lax.fori_loop(0, total // chunk, share, (zero, zero))
    up_part[0] = sum_q
    up_part[1] = sum_v

    def back(step, other):
        return to_member(back_out.at[other], back_in.at[step - 1], b_send, b_recv, other)

    for step in range(1, members):
        back(step, others[step]).start()
    owner = lax.div(me, members // groups)
    up_move = to_group(up_part, up_in.at[dp], u_send.at[dp], u_recv.at[dp], owner)

    @pl.when(owner != dp)
    def _():
        up_move.start()

    start_bulk(0, far)

    slots = members - 1
    backs = bytes_of(back_in.at[pl.ds(0, slots)], b_send, b_recv, others[1])
    backs.wait_recv()
    back_low = jnp.sum(back_in[0:slots], axis=0) + back_out[me]
    back_low = back_low.astype(BF16)

    def fill(group):
        cols = pl.ds(pl.multiple_of(group * d_cols, 128), d_cols)
        part[group] = jnp.dot(back_low, hid[:, cols], preferred_element_type=F32)

    def exchange(step):
        other = across(step)
        return to_group(part.at[other], z_in.at[step], z_send.at[step], z_recv.at[step], other)

    for step in range(1, groups):
        fill(across(step))
        exchange(step).start()
    start_bulk(1, near)
    start_bulk(1, far)
    fill(dp)

    def place_of(member):
        return pl.ds(n_tiles + 2 * lax.rem(member, members // groups), 2)

    def spread_up(step, other):
        mine = done.at[place_of(me)]
        return to_member(mine, mine, c_send, c_recv, other)

    @pl.when(owner == dp)
    def _():
        summed = up_part[...]
        for step in range(1, groups):
            source = across(step)
            to_group(up_part, up_in.at[source], u_send.at[source], u_recv.at[source], source).wait_recv()
            summed = summed + up_in[source]
        done[place_of(me)] = summed * ADAPTER_SCALE

        for step in range(1, members):
            spread_up(step, others[step]).start()

    down = part[dp]
    for step in range(1, groups):
        exchange(step).wait()
        down = down + z_in[step]
    for tile in range(n_tiles):
        column, half = tile // 2, tile % 2
        tiles[tile] = down[half * 8:half * 8 + 8, column * 128:(column + 1) * 128]

    def scatter(step, other):
        return to_member(
            tiles.at[lax.rem(other, n_tiles)], r_in.at[step - 1], r_send, r_recv, other
        )

    def spread(step, other):
        mine = done.at[lax.rem(me, n_tiles)]
        return to_member(mine, mine, a_send, a_recv, other)

    for step in range(1, members):
        @pl.when(others[step] < n_tiles)
        def _(step=step):
            scatter(step, others[step]).start()

    start_bulk(2, near)

    @pl.when(me < n_tiles)
    def _():
        bytes_of(r_in, r_send, r_recv, others[1]).wait_recv()
        done[me] = (tiles[me] + jnp.sum(r_in[...], axis=0)) * ADAPTER_SCALE
        for step in range(1, members):
            spread(step, others[step]).start()

    start_bulk(2, far)

    backs.wait_send()

    @pl.when(me < n_tiles)
    def _():
        bytes_of(tiles.at[pl.ds(0, n_tiles - 1)], r_send, r_recv, others[1]).wait_send()
        bytes_of(r_in, a_send, a_recv, others[1]).wait_send()
        bytes_of(tiles.at[pl.ds(0, n_tiles - 1)], a_send, a_recv, others[1]).wait_recv()

    @pl.when(me >= n_tiles)
    def _():
        bytes_of(tiles, r_send, r_recv, others[1]).wait_send()
        bytes_of(tiles, a_send, a_recv, others[1]).wait_recv()

    per_group = members // groups

    @pl.when(owner == dp)
    def _():
        bytes_of(back_in.at[pl.ds(0, slots)], c_send, c_recv, others[1]).wait_send()
        bytes_of(up_in.at[pl.ds(0, per_group - 1)], c_send, c_recv, others[1]).wait_recv()

    @pl.when(owner != dp)
    def _():
        bytes_of(up_in.at[pl.ds(0, per_group)], c_send, c_recv, others[1]).wait_recv()

    for index, (_, dst) in enumerate(pairs):
        bytes_of(dst.at[:, pl.ds(0, slots * HD)], send.at[index], recv.at[index], others[1]).wait()

    @pl.when(owner != dp)
    def _():
        up_move.wait_send()

    for copy in own:
        copy.wait()


def return_heads(dq, dk, dv, table, low, hidden, up_query, up_value):
    rows, model = hidden.shape
    total = dq.shape[0]
    width = up_query.shape[1]
    vmem = pl.BlockSpec(memory_space=pltpu.VMEM)
    grad = jax.ShapeDtypeStruct((rows, width), BF16)
    d_cols = model // 8
    n_tiles = 2 * d_cols // 128
    all_tiles = n_tiles + 2 * (width // 8) // 128
    dma = pltpu.SemaphoreType.DMA
    return pl.pallas_call(
        return_kernel,
        name="return_heads",
        out_shape=(grad, grad, grad, jax.ShapeDtypeStruct((all_tiles, 8, 128), F32)),
        in_specs=[vmem] * 8,
        out_specs=[vmem] * 4,
        scratch_shapes=[
            pltpu.VMEM((32, 2 * RANK, rows), F32),
            pltpu.VMEM((32, 2 * RANK, rows), F32),
            pltpu.VMEM((8, 2 * RANK, d_cols), F32),
            pltpu.VMEM((8, 2 * RANK, d_cols), F32),
            pltpu.VMEM((2, RANK, HD), F32),
            pltpu.VMEM((8, 2, RANK, HD), F32),
            pltpu.VMEM((n_tiles, 8, 128), F32),
            pltpu.VMEM((31, 8, 128), F32),
            dma((3,)), dma((3,)), dma((3,)),
            dma, dma,
            dma((8,)), dma((8,)),
            dma((8,)), dma((8,)),
            dma, dma,
            dma, dma,
            dma, dma,
        ],
        compiler_params=pltpu.CompilerParams(
            collective_id=1, has_side_effects=True, vmem_limit_bytes=16 << 20
        ),
    )(dq, dk, dv, table, low, hidden, up_query, up_value)


def finish_kernel(gq, gk, gv, done, oq, ok, ov, qd, qu, vd, vu, sems):
    copies = [
        pltpu.make_async_copy(src, dst, sems.at[index])
        for index, (src, dst) in enumerate(((gq, oq), (gk, ok), (gv, ov)))
    ]
    for copy in copies:
        copy.start()
    d_tiles = qd.shape[1] // 128
    for column in range(d_tiles):
        cols = slice(column * 128, (column + 1) * 128)
        qd[:, cols] = done[2 * column]
        vd[:, cols] = done[2 * column + 1]
    for column in range(qu.shape[1] // 128):
        cols = slice(column * 128, (column + 1) * 128)
        qu[:, cols] = done[2 * (d_tiles + column)]
        vu[:, cols] = done[2 * (d_tiles + column) + 1]
    for copy in copies:
        copy.wait()


def write_results(gq, gk, gv, done, model):
    rows, width = gq.shape
    vmem = pl.BlockSpec(memory_space=pltpu.VMEM)
    hbm = pl.BlockSpec(memory_space=pltpu.HBM)
    grad = jax.ShapeDtypeStruct((rows, width), BF16)
    down = jax.ShapeDtypeStruct((RANK, model // 8), F32)
    up = jax.ShapeDtypeStruct((RANK, width // 8), F32)
    return pl.pallas_call(
        finish_kernel,
        name="write_results",
        out_shape=(grad, grad, grad, down, up, down, up),
        in_specs=[vmem] * 4,
        out_specs=[hbm] * 3 + [vmem] * 4,
        scratch_shapes=[pltpu.SemaphoreType.DMA((3,))],
        compiler_params=pltpu.CompilerParams(vmem_limit_bytes=4 << 20),
    )(gq, gk, gv, done)


def shards(
    hidden,
    queries,
    key_states,
    value_states,
    attention_out,
    grad_out,
    lengths,
    down_query,
    up_query,
    down_value,
    up_value,
):
    q, k, v, g, delta, low, lse, kt, table = gather_heads(
        lengths, queries, key_states, value_states, grad_out, attention_out, hidden, down_query, down_value
    )
    dq, dk, dv = attention_backward(lengths, q, k, v, g, delta, lse, kt)
    gq, gk, gv, done = return_heads(dq, dk, dv, table, low, hidden, up_query, up_value)
    return write_results(gq, gk, gv, done, hidden.shape[1])


def solution(mesh):
    tokens = P(("dp", "seq"), None)
    return jax.shard_map(
        shards,
        mesh=mesh,
        in_specs=(tokens,) * 6 + (P("dp", None), P(), P(), P(), P()),
        out_specs=(tokens,) * 3 + (P(None, "dp"),) * 4,
        check_vma=False,
    )
```
